256 devices in a mesh: segment: 2 (over core), expert: 128 (over z, y, x).
Axes of the slice: x: 4, y: 4, z: 8, core: 2. Of those that a mesh axis runs over, the one named last changes fastest.
Arguments:
- saved_input: bfloat16 [2, 2, 8192, 2048], P('segment', None, 'expert'), may hold values from -6 to 6
- out_grad: bfloat16 [2, 8192, 2048], P(None, 'expert'), may hold values from -6 to 6
- expert_ids: int32 [2, 2, 8192, 2], P('segment', None, 'expert'), may hold values from 0 to 127, all different within a row; in each aligned block of 64 rows (0 to 63, 64 to 127, ..., all dimensions but the last counted through in order) at most 2 rows name the same one
- router_weights: float32 [2, 2, 8192, 2], P('segment', None, 'expert'), may hold values from 0.1 to 0.9
- w_gate: bfloat16 [2, 128, 2048, 384], P('segment', 'expert'), may hold values from -0.125 to 0.125
- w_up: bfloat16 [2, 128, 2048, 384], P('segment', 'expert'), may hold values from -0.125 to 0.125
- w_down: bfloat16 [2, 128, 384, 2048], P('segment', 'expert'), may hold values from -0.3125 to 0.3125
- eigenbasis: bfloat16 [2, 128, 384, 384], P('segment', 'expert'), may hold values from -0.3125 to 0.3125
Outputs:
- input_grad: bfloat16 [2, 2, 8192, 2048], P('segment', None, 'expert')
- rotated_grad: bfloat16 [2, 128, 384, 2048], P('segment', 'expert')
- ekfac_scales: float32 [2, 128, 384, 2048], P('segment', 'expert')
The draws below stay inside these ranges and needn't reach their ends.
Inputs may be any that keep to these rules, and one draw needn't show every extreme that they name: `expert_ids`: the two experts of a token differ. In each layer and micro-batch, at most 2 rows of one block of 64 tokens choose the same expert, and some block reaches 2.
All inputs are finite; a program needn't handle non-finite values.
Results may differ from the reference program's by a relative error of at most 0.0085.
Values may be sent and summed in bfloat16 or wider, within the bound.
No kernel may reach another device: no remote copies, remote signals or barrier semaphores. Data moves between devices by JAX's collectives and lax.ppermute only.
A program may use at most 128 MiB of HBM per device.

```python
import math
import jax
import jax.numpy as jnp
import numpy as np
from jax import lax

D = 2048
FF = 384
M = 2
TOK_TICK = 64
EXPERTS = 128
LAYERS = 2
TOKENS = 8192
CAP = 2
N_EXPERT = 128


def level_of(rng, extent, cuts, smallest, top_value):
    factor_of = 1.0
    for axis_at, parts in cuts:
        steps = jax.random.uniform(jax.random.fold_in(jax.random.fold_in(rng, 6), axis_at), (parts,), jnp.float32, smallest / len(cuts), top_value / len(cuts))
        factor_of = factor_of * jnp.repeat(jnp.exp(steps), extent[axis_at] // parts).reshape((-1,) + (1,) * (len(extent) - 1 - axis_at))
    return factor_of


def routed_block(own_key, own, number, rows, count, top, limit, lean):
    order = jax.random.permutation(own_key, count)
    packed, usual = portions_of(count, rows * top, limit, lean, True), portions_of(count, rows * top, limit, lean, False)
    places = jnp.arange(count)

    def named(tallies, turn):
        used = int((tallies > 0).sum())
        fixed = max(1, used // 4)
        moved = fixed + (places - fixed + turn * (used - fixed)) % max(1, count - fixed)
        return jnp.zeros((count,), jnp.int32).at[order[jnp.where(places < fixed, places, moved)]].set(jnp.asarray(tallies, jnp.int32))

    tallies = jnp.where(number % 4 == 0, named(packed, number // 4), named(usual, number - number // 4 - 1))
    mixed = jax.random.permutation(jax.random.fold_in(own, 3), count)
    giver, receiver = mixed[0:count // 2 * 2:2], mixed[1:count // 2 * 2:2]
    margin = jnp.minimum(tallies[giver] - 1, limit - tallies[receiver]) // 2
    margin = jnp.where((giver == order[0]) | (receiver == order[0]) | (tallies[receiver] == 0), 0, jnp.maximum(margin, 0))
    moved = jax.random.randint(jax.random.fold_in(own, 4), (count // 2,), 0, 1 << 20) % (margin + 1)
    tallies = tallies.at[giver].add(-moved).at[receiver].add(moved)
    labels = jnp.searchsorted(jnp.cumsum(tallies), jnp.arange(rows * top), side="right").astype(jnp.int32)
    table = labels.reshape(top, rows).T
    table = table[jax.random.permutation(jax.random.fold_in(own, 1), rows)]
    turn = jax.random.randint(jax.random.fold_in(own, 2), (rows, 1), 0, top)
    return jnp.take_along_axis(table, (jnp.arange(top)[None, :] + turn) % top, axis=1)


def portions_of(count, total, bound, lean, full):
    portions = [(1 << 20) // math.isqrt(standing ** lean) + 1 for standing in range(1, count + 1)]
    largest = bound if full else min(bound, max(-(-total // count), total * portions[0] // sum(portions)))
    least = 1 if total - largest >= count - 1 else 0
    holding, spare = [largest] + [least] * (count - 1), total - largest - least * (count - 1)
    while spare > 0:
        candidates = [i for i in range(1, count) if holding[i] < largest] or [i for i in range(1, count) if holding[i] < bound]
        whole, remaining = sum([portions[i] for i in candidates]), spare
        for i in candidates:
            extra = min(bound - holding[i], max(1, remaining * portions[i] // whole), spare)
            holding[i] = holding[i] + extra
            spare = spare - extra
    return np.array(holding)


def scatter_about(key, shape, width, bound, shards=(), kind=jnp.bfloat16):
    values = jax.random.normal(key, shape, jnp.float32) * width
    if len(shards) > 0:
        values = level_of(key, shape, shards, -0.22, 0.18) * values
    return jnp.clip(values, min=-bound, max=bound).astype(kind)


def setup_inputs(seed: int = 0) -> dict:
    key_of = jax.random.split(jax.random.key(seed), 9)
    saved_input = scatter_about(key_of[0], (LAYERS, M, TOKENS, D), 1.0, 6.0, ((0, 2), (2, 128)))
    out_grad = scatter_about(key_of[1], (M, TOKENS, D), 1.0, 6.0, ((1, 128),))
    expert_ids_keys = jax.random.split(jax.random.fold_in(key_of[2], 1), LAYERS * M * TOKENS // TOK_TICK)
    expert_ids_turns = jax.random.permutation(jax.random.fold_in(key_of[2], 3), LAYERS * M * TOKENS // TOK_TICK)
    expert_ids = jax.vmap(lambda own, number: routed_block(jax.random.fold_in(key_of[2], 2), own, number, TOK_TICK, EXPERTS, 2, CAP, 2))(expert_ids_keys, expert_ids_turns).reshape((LAYERS, M, TOKENS, 2))
    router_weights = jnp.clip(0.1 + 0.79999997 * jax.random.uniform(key_of[3], (LAYERS, M, TOKENS, 2), jnp.float32) ** level_of(key_of[3], (LAYERS, M, TOKENS, 2), ((0, 2), (2, 128)), -0.2, 0.2), 0.1, 0.9)
    w_gate = scatter_about(key_of[4], (LAYERS, EXPERTS, D, FF), D ** -0.5, 0.125, ((0, 2), (1, 128)))
    w_up = scatter_about(key_of[5], (LAYERS, EXPERTS, D, FF), D ** -0.5, 0.125, ((0, 2), (1, 128)))
    w_down = scatter_about(key_of[6], (LAYERS, EXPERTS, FF, D), FF ** -0.5, 0.3125, ((0, 2), (1, 128)))
    eigenbasis = scatter_about(key_of[7], (LAYERS, EXPERTS, FF, FF), FF ** -0.5, 0.3125, ((0, 2), (1, 128)))
    return {"saved_input": saved_input, "out_grad": out_grad, "expert_ids": expert_ids, "router_weights": router_weights, "w_gate": w_gate, "w_up": w_up, "w_down": w_down, "eigenbasis": eigenbasis}


def silu_parts(hidden_gate):
    sigma = jax.nn.sigmoid(hidden_gate)
    return hidden_gate * sigma, sigma * (1.0 + hidden_gate * (1.0 - sigma))


def expert_backward(inputs):
    x_rows, dy_rows, gate_mat, up_mat, down_mat, basis = inputs
    hidden_gate = jnp.dot(x_rows, gate_mat, preferred_element_type=jnp.float32)
    hidden_up = jnp.dot(x_rows, up_mat, preferred_element_type=jnp.float32)
    act, dact = silu_parts(hidden_gate)
    activ = (act * hidden_up).astype(jnp.bfloat16)
    grad_act = lax.dot_general(dy_rows, down_mat, (((1,), (1,)), ((), ())), preferred_element_type=jnp.float32)
    grad_gate = (grad_act * hidden_up * dact).astype(jnp.bfloat16)
    grad_up = (grad_act * act).astype(jnp.bfloat16)
    dx_rows = (lax.dot_general(grad_gate, gate_mat, (((1,), (1,)), ((), ())), preferred_element_type=jnp.float32)
               + lax.dot_general(grad_up, up_mat, (((1,), (1,)), ((), ())), preferred_element_type=jnp.float32)).astype(jnp.bfloat16)
    rotated = jnp.dot(activ, basis, preferred_element_type=jnp.float32).astype(jnp.bfloat16)
    grad_term = lax.dot_general(rotated, dy_rows, (((0,), (0,)), ((), ())), preferred_element_type=jnp.float32)
    rot_sq = (rotated.astype(jnp.float32) ** 2).astype(jnp.bfloat16)
    dy_sq = (dy_rows.astype(jnp.float32) ** 2).astype(jnp.bfloat16)
    scale_term = lax.dot_general(rot_sq, dy_sq, (((0,), (0,)), ((), ())), preferred_element_type=jnp.float32)
    return dx_rows, grad_term, scale_term


def slot_of(ids):
    flat = ids.reshape(N_EXPERT, TOK_TICK * 2)
    onehot = (flat[:, :, None] == jnp.arange(EXPERTS, dtype=jnp.int32)[None, None, :]).astype(jnp.int32)
    prior = jnp.cumsum(onehot, axis=1) - onehot
    rank = jnp.sum(prior * onehot, axis=2)
    source = jnp.arange(N_EXPERT, dtype=jnp.int32)[:, None]
    return (source * CAP + rank).reshape(-1).astype(jnp.int32)


def reference(saved_input, out_grad, expert_ids, router_weights, w_gate, w_up, w_down, eigenbasis):
    buffer_rows = N_EXPERT * CAP
    grads_in = [None] * LAYERS
    grad_sums = [None] * LAYERS
    scale_sums = [None] * LAYERS
    incoming = out_grad
    for layer in reversed(range(LAYERS)):
        grad_acc = jnp.zeros((EXPERTS, FF, D), jnp.float32)
        scale_acc = jnp.zeros((EXPERTS, FF, D), jnp.float32)
        layer_out = []
        for micro in range(M):
            tokens_in = saved_input[layer, micro]
            upstream = incoming[micro]
            ids = expert_ids[layer, micro]
            slots = slot_of(ids)
            flat_ids = ids.reshape(-1).astype(jnp.int32)
            x_rep = jnp.repeat(tokens_in, 2, axis=0)
            dy_rep = (router_weights[layer, micro].reshape(-1, 1) * jnp.repeat(upstream.astype(jnp.float32), 2, axis=0)).astype(jnp.bfloat16)
            x_buf = jnp.zeros((EXPERTS, buffer_rows, D), jnp.bfloat16).at[flat_ids, slots].set(x_rep)
            dy_buf = jnp.zeros((EXPERTS, buffer_rows, D), jnp.bfloat16).at[flat_ids, slots].set(dy_rep)
            dx_buf, grad_term, scale_term = lax.map(expert_backward, (x_buf, dy_buf, w_gate[layer], w_up[layer], w_down[layer], eigenbasis[layer]))
            grad_acc = grad_acc + grad_term
            scale_acc = scale_acc + scale_term
            back = dx_buf[flat_ids, slots].astype(jnp.float32).reshape(TOKENS, 2, D)
            layer_out.append((upstream.astype(jnp.float32) + back[:, 0] + back[:, 1]).astype(jnp.bfloat16))
        grads_in[layer] = jnp.stack(layer_out)
        incoming = grads_in[layer]
        grad_sums[layer] = (grad_acc * (1.0 / M)).astype(jnp.bfloat16)
        scale_sums[layer] = scale_acc * (1.0 / M)
    return (jnp.stack(grads_in), jnp.stack(grad_sums), jnp.stack(scale_sums))
```

```python
import functools
import jax
import jax.numpy as jnp
from jax import lax
from jax.experimental import pallas as pl
from jax.experimental.pallas import tpu as pltpu
from jax.sharding import PartitionSpec as P

LANES = 128
CAP = 2
F32 = jnp.float32
BF16 = jnp.bfloat16
SMEM = pl.BlockSpec(memory_space=pltpu.SMEM)
VMEM = pl.BlockSpec(memory_space=pltpu.VMEM)


def rows_to_tiles(rows, tiles, count, depth):
    for j in range(depth):
        tiles[pl.ds(j, count, stride=depth), :] = rows[:, j * LANES : (j + 1) * LANES]


def tiles_to_rows(tiles, rows, count, depth):
    for j in range(depth):
        rows[:, j * LANES : (j + 1) * LANES] = tiles[pl.ds(j, count, stride=depth), :].astype(
            rows.dtype
        )


def clear(send, experts):
    zero = jnp.zeros(send.shape[1:], send.dtype)

    def one(e, carry):
        send[e] = zero
        return carry

    lax.fori_loop(0, experts, one, 0, unroll=4)


def dispatch_kernel(
    here, own_ids, other_ids, own_w, other_w, own_x, other_x, grad, send, slots, grad_tiles,
    x_upper, x_lower, g_tiles, counts,
):
    tokens, width = grad.shape
    depth = width // LANES
    experts = send.shape[0]
    upper = here[0] == 1
    own = own_x[...].astype(F32)
    other = other_x[...].astype(F32)
    rows_to_tiles(jnp.where(upper, own, other), x_upper, tokens, depth)
    rows_to_tiles(jnp.where(upper, other, own), x_lower, tokens, depth)
    rows_to_tiles(grad[...].astype(F32), g_tiles, tokens, depth)
    clear(send, experts)

    def reset(e, carry):
        counts[0, e] = 0
        counts[1, e] = 0
        return carry

    lax.fori_loop(0, experts, reset, 0, unroll=8)

    def token(t, carry):
        at = pl.ds(pl.multiple_of(t * depth, depth), depth)
        up = x_upper[at, :].astype(BF16)
        low = x_lower[at, :].astype(BF16)
        g = g_tiles[at, :]
        grad_tiles[t] = g.astype(BF16)
        for k in range(2):
            p = 2 * t + k
            mine, theirs = own_ids[p], other_ids[p]
            e1 = jnp.where(upper, mine, theirs)
            e0 = jnp.where(upper, theirs, mine)
            c1 = jnp.minimum(counts[0, e1], CAP - 1)
            c0 = jnp.minimum(counts[1, e0], CAP - 1)
            counts[0, e1] = c1 + 1
            counts[1, e0] = c0 + 1
            slots[0, p] = e0 * CAP + c0
            slots[1, p] = e1 * CAP + c1
            weight = jnp.where(upper, own_w[p], other_w[p])
            send[e1, c1] = up
            send[e1, CAP + c1] = (weight * g).astype(BF16)
            send[e0, 2 * CAP + c0] = low
        return carry

    lax.fori_loop(0, tokens, token, 0)


def relay_kernel(here, slots, own_w, other_w, back, upstream, send, grad_out):
    tokens = upstream.shape[0]
    experts = send.shape[0]
    upper = here[0] == 1
    clear(send, experts)

    def token(t, carry):
        total = upstream[t].astype(F32)
        for k in range(2):
            s = slots[1, 2 * t + k]
            total = total + back[s // CAP, s % CAP].astype(F32)
        rounded = total.astype(BF16)
        grad_out[t] = rounded
        g = rounded.astype(F32)
        for k in range(2):
            p = 2 * t + k
            s = slots[0, p]
            weight = jnp.where(upper, other_w[p], own_w[p])
            send[s // CAP, s % CAP] = (weight * g).astype(BF16)
        return carry

    lax.fori_loop(0, tokens, token, 0)


def finish_kernel(here, slots, back, upstream, keep, away, low, up):
    tokens, depth = upstream.shape[0], upstream.shape[1]
    upper = here[0] == 1

    def token(t, carry):
        at = pl.ds(pl.multiple_of(t * depth, depth), depth)
        g = upstream[t].astype(F32)
        up[at, :] = g
        total = g
        for k in range(2):
            s = slots[0, 2 * t + k]
            total = total + back[s // CAP, s % CAP].astype(F32)
        low[at, :] = total
        return carry

    lax.fori_loop(0, tokens, token, 0)
    for j in range(depth):
        columns = slice(j * LANES, (j + 1) * LANES)
        high = up[pl.ds(j, tokens, stride=depth), :]
        down = low[pl.ds(j, tokens, stride=depth), :]
        keep[:, columns] = jnp.where(upper, high, down).astype(BF16)
        away[:, columns] = jnp.where(upper, down, high).astype(BF16)


def untile(block, tiles, rows):
    experts, cap, depth, lanes = block.shape
    count = experts * cap
    tiles[...] = block[...].astype(F32).reshape(count * depth, lanes)
    tiles_to_rows(tiles, rows, count, depth)


def forward_parts(rows, gate_up):
    hidden = jnp.dot(rows, gate_up, preferred_element_type=F32)
    half = hidden.shape[1] // 2
    gate, up = hidden[:, :half], hidden[:, half:]
    sigma = 1.0 / (1.0 + jnp.exp(-gate))
    act = gate * sigma
    dact = sigma * (1.0 + gate * (1.0 - sigma))
    return act, up * dact, (act * up).astype(BF16)


def backward_parts(act, slope, dy_rows, down_t, gate_up_t, tiles, send):
    experts, cap, depth, lanes = send.shape
    count = experts * cap
    grad_act = jnp.dot(dy_rows[...], down_t[...], preferred_element_type=F32)
    both = jnp.concatenate(
        [(grad_act * slope).astype(BF16), (grad_act * act).astype(BF16)], axis=1
    )
    dx = jnp.dot(both, gate_up_t[...], preferred_element_type=F32)
    rows_to_tiles(dx, tiles, count, depth)
    send[...] = tiles[...].reshape(experts, cap, depth, lanes).astype(BF16)


def upper_kernel(x, dy, gate_up, down_t, gate_up_t, send, dy_rows, activ, tiles, x_rows):
    untile(x, tiles, x_rows)
    act, slope, rounded = forward_parts(x_rows[...], gate_up[...])
    activ[...] = rounded
    untile(dy, tiles, dy_rows)
    backward_parts(act, slope, dy_rows, down_t, gate_up_t, tiles, send)


def forward_kernel(x, gate_up, act_out, slope_out, activ, tiles, x_rows):
    untile(x, tiles, x_rows)
    act, slope, rounded = forward_parts(x_rows[...], gate_up[...])
    act_out[...] = act
    slope_out[...] = slope
    activ[...] = rounded


def lower_kernel(dy, act, slope, down_t, gate_up_t, send, dy_rows, tiles):
    untile(dy, tiles, dy_rows)
    backward_parts(act[...], slope[...], dy_rows, down_t, gate_up_t, tiles, send)


def whole(block, at):
    return pl.BlockSpec(block, lambda i: at)


def call(kernel, args, in_specs, out_shape, out_specs, scratch, flops, moved):
    return pl.pallas_call(
        kernel,
        grid=(1,),
        in_specs=in_specs,
        out_shape=out_shape,
        out_specs=out_specs,
        scratch_shapes=scratch,
        compiler_params=pltpu.CompilerParams(vmem_limit_bytes=48 * 1024 * 1024),
        cost_estimate=pl.CostEstimate(flops=flops, bytes_accessed=moved, transcendentals=0),
    )(*args)


def swapped(block):
    return lax.ppermute(block, "segment", [(0, 1), (1, 0)])


def exchanged(block):
    return lax.all_to_all(block, "expert", split_axis=0, concat_axis=0, tiled=True)


def shape(dims, kind=BF16):
    return jax.ShapeDtypeStruct(dims, kind)


def shards(saved_input, out_grad, expert_ids, router_weights, w_gate, w_up, w_down, eigenbasis):
    experts = lax.axis_size("expert")
    segment = lax.axis_index("segment")
    upper = segment == 1
    micros, tokens, width = saved_input.shape[1:]
    hidden = w_gate.shape[-1]
    depth = width // LANES
    count = experts * CAP
    here = segment.astype(jnp.int32).reshape(1)

    ids = expert_ids[0].reshape(micros, tokens * 2)
    weights = router_weights[0].reshape(micros, tokens * 2)
    mine = functools.partial(lax.dynamic_index_in_dim, index=segment, axis=0, keepdims=False)
    theirs = functools.partial(lax.dynamic_index_in_dim, index=1 - segment, axis=0, keepdims=False)
    own_ids, other_ids = mine(ids), swapped(theirs(ids))
    own_w, other_w = mine(weights), swapped(theirs(weights))
    own_x, other_x = mine(saved_input[0]), swapped(theirs(saved_input[0]))
    grad = mine(out_grad)

    tile_rows = tokens * depth
    send, slots, grad_tiles = call(
        dispatch_kernel,
        (here, own_ids, other_ids, own_w, other_w, own_x, other_x, grad),
        [SMEM] * 5 + [VMEM] * 3,
        (
            shape((experts, 3 * CAP, depth, LANES)),
            shape((2, tokens * 2), jnp.int32),
            shape((tokens, depth, LANES)),
        ),
        (VMEM, SMEM, VMEM),
        [pltpu.VMEM((tile_rows, LANES), F32)] * 3 + [pltpu.SMEM((2, experts), jnp.int32)],
        1_000_000,
        5_000_000,
    )
    arrived = exchanged(send)

    other_gate, other_up = swapped(w_gate[0, 0]), swapped(w_up[0, 0])
    other_down, other_basis = swapped(w_down[0, 0]), swapped(eigenbasis[0, 0])

    def of_layer(layer):
        here_now = segment == layer
        gate = jnp.where(here_now, w_gate[0, 0], other_gate)
        up = jnp.where(here_now, w_up[0, 0], other_up)
        down = jnp.where(here_now, w_down[0, 0], other_down)
        basis = jnp.where(here_now, eigenbasis[0, 0], other_basis)
        gate_up = jnp.concatenate([gate, up], axis=1)
        return gate_up, down.T, gate_up.T, basis

    gate_up1, down_t1, gate_up_t1, basis1 = of_layer(1)
    gate_up0, down_t0, gate_up_t0, basis0 = of_layer(0)

    part = (experts, CAP, depth, LANES)
    tiles = pltpu.VMEM((count * depth, LANES), F32)
    rows = pltpu.VMEM((count, width), BF16)
    mat = 2 * count * width * hidden
    back_send, dy_rows1, activ1 = call(
        upper_kernel,
        (arrived, arrived, gate_up1, down_t1, gate_up_t1),
        [whole(part, (0, 0, 0, 0)), whole(part, (0, 1, 0, 0))] + [VMEM] * 3,
        (shape(part), shape((count, width)), shape((count, hidden))),
        (VMEM,) * 3,
        [tiles, rows],
        5 * mat,
        9_000_000,
    )
    back = exchanged(back_send)
    act0, slope0, activ0 = call(
        forward_kernel,
        (arrived, gate_up0),
        [whole(part, (0, 2, 0, 0)), VMEM],
        (shape((count, hidden), F32), shape((count, hidden), F32), shape((count, hidden))),
        (VMEM,) * 3,
        [tiles, rows],
        2 * mat,
        5_000_000,
    )
    rotated1 = jnp.dot(activ1, basis1, preferred_element_type=F32).astype(BF16)
    rotated0 = jnp.dot(activ0, basis0, preferred_element_type=F32).astype(BF16)

    dy_send, grad1 = call(
        relay_kernel,
        (here, slots, own_w, other_w, back, grad_tiles),
        [SMEM] * 4 + [VMEM] * 2,
        (shape(part), shape((tokens, depth, LANES))),
        (VMEM,) * 2,
        [],
        1_000_000,
        3_000_000,
    )
    dy = exchanged(dy_send)
    back_send0, dy_rows0 = call(
        lower_kernel,
        (dy, act0, slope0, down_t0, gate_up_t0),
        [VMEM] * 5,
        (shape(part), shape((count, width))),
        (VMEM,) * 2,
        [tiles],
        3 * mat,
        8_000_000,
    )
    back0 = exchanged(back_send0)

    all_rotated = jnp.concatenate(
        [
            jnp.where(upper, rotated1, rotated0),
            swapped(jnp.where(upper, rotated0, rotated1)),
        ],
        axis=0,
    )
    all_dy = jnp.concatenate(
        [
            jnp.where(upper, dy_rows1, dy_rows0),
            swapped(jnp.where(upper, dy_rows0, dy_rows1)),
        ],
        axis=0,
    )
    rot_sq = (all_rotated.astype(F32) ** 2).astype(BF16)
    dy_sq = (all_dy.astype(F32) ** 2).astype(BF16)
    over_rows = (((0,), (0,)), ((), ()))
    grad_sum = lax.dot_general(all_rotated, all_dy, over_rows, preferred_element_type=F32)
    scale_sum = lax.dot_general(rot_sq, dy_sq, over_rows, preferred_element_type=F32)
    rotated_grad = (grad_sum * (1.0 / micros)).astype(BF16)
    ekfac_scales = scale_sum * (1.0 / micros)

    keep, away = call(
        finish_kernel,
        (here, slots, back0, grad1),
        [SMEM] * 2 + [VMEM] * 2,
        (shape((tokens, width)), shape((tokens, width))),
        (VMEM,) * 2,
        [pltpu.VMEM((tile_rows, LANES), F32)] * 2,
        1_000_000,
        2_000_000,
    )
    came = swapped(away)
    grads = jnp.stack([jnp.where(upper, came, keep), jnp.where(upper, keep, came)])
    return (grads[None], rotated_grad[None, None], ekfac_scales[None, None])


def solution(mesh):
    in_specs = (
        P("segment", None, "expert", None),
        P(None, "expert", None),
        P("segment", None, "expert", None),
        P("segment", None, "expert", None),
        P("segment", "expert", None, None),
        P("segment", "expert", None, None),
        P("segment", "expert", None, None),
        P("segment", "expert", None, None),
    )
    out_specs = (
        P("segment", None, "expert", None),
        P("segment", "expert", None, None),
        P("segment", "expert", None, None),
    )
    return jax.shard_map(shards, mesh=mesh, in_specs=in_specs, out_specs=out_specs, check_vma=False)
```

```python
import functools
import jax
import jax.numpy as jnp
from jax import lax
from jax.experimental import pallas as pl
from jax.experimental.pallas import tpu as pltpu
from jax.sharding import PartitionSpec as P

LANES = 128
CAP = 2
F32 = jnp.float32
BF16 = jnp.bfloat16
SMEM = pl.BlockSpec(memory_space=pltpu.SMEM)
VMEM = pl.BlockSpec(memory_space=pltpu.VMEM)
HBM = pl.BlockSpec(memory_space=pltpu.HBM)


def rows_to_tiles(rows, tiles, count, depth):
    for j in range(depth):
        tiles[pl.ds(j, count, stride=depth), :] = rows[:, j * LANES : (j + 1) * LANES]


def tiles_to_rows(tiles, rows, count, depth):
    for j in range(depth):
        rows[:, j * LANES : (j + 1) * LANES] = tiles[pl.ds(j, count, stride=depth), :].astype(
            rows.dtype
        )


def clear(send, experts):
    zero = jnp.zeros(send.shape[1:], send.dtype)

    def one(e, carry):
        send[e] = zero
        return carry

    lax.fori_loop(0, experts, one, 0, unroll=8)


def on_core(which):
    return lax.axis_index("segment") == which


def fetch(source, target, sem):
    copy = pltpu.make_async_copy(source, target, sem)
    copy.start()
    return copy


def fetch_one_of(first, own, other, target, sem):
    @pl.when(first)
    def _():
        pltpu.make_async_copy(own, target, sem).start()

    @pl.when(jnp.logical_not(first))
    def _():
        pltpu.make_async_copy(other, target, sem).start()

    return pltpu.make_async_copy(own, target, sem)


def dispatch_kernel(
    own_ids, other_ids, own_w, other_w, own_x, other_x, grad, after, sent, slots, grad_tiles,
    send, x_upper, x_lower, g_tiles, counts, sems,
):
    tokens, width = grad.shape
    depth = width // LANES
    experts = send.shape[0]
    upper = on_core(1)
    own = own_x[...].astype(F32)
    other = other_x[...].astype(F32)
    rows_to_tiles(jnp.where(upper, own, other), x_upper, tokens, depth)
    rows_to_tiles(jnp.where(upper, other, own), x_lower, tokens, depth)
    rows_to_tiles(grad[...].astype(F32), g_tiles, tokens, depth)
    clear(send, experts)

    def reset(e, carry):
        counts[0, e] = 0
        counts[1, e] = 0
        return carry

    lax.fori_loop(0, experts, reset, 0, unroll=8)

    def first(t, carry):
        at = pl.ds(pl.multiple_of(t * depth, depth), depth)
        row = x_upper[at, :].astype(BF16)
        g = g_tiles[at, :]
        grad_tiles[t] = g.astype(BF16)
        for k in range(2):
            p = 2 * t + k
            e = jnp.where(upper, own_ids[p], other_ids[p])
            c = jnp.minimum(counts[0, e], CAP - 1)
            counts[0, e] = c + 1
            slots[1, p] = e * CAP + c
            weight = jnp.where(upper, own_w[p], other_w[p])
            send[e, c] = row
            send[e, CAP + c] = (weight * g).astype(BF16)
        return carry

    lax.fori_loop(0, tokens, first, 0, unroll=2)
    urgent = fetch(send.at[:, : 2 * CAP], sent.at[:, : 2 * CAP], sems.at[0])

    def second(t, carry):
        at = pl.ds(pl.multiple_of(t * depth, depth), depth)
        row = x_lower[at, :].astype(BF16)
        for k in range(2):
            p = 2 * t + k
            e = jnp.where(upper, other_ids[p], own_ids[p])
            c = jnp.minimum(counts[1, e], CAP - 1)
            counts[1, e] = c + 1
            slots[0, p] = e * CAP + c
            send[e, 2 * CAP + c] = row
        return carry

    lax.fori_loop(0, tokens, second, 0, unroll=2)
    rest = fetch(send.at[:, 2 * CAP :], sent.at[:, 2 * CAP :], sems.at[1])
    urgent.wait()
    rest.wait()


def relay_kernel(slots, own_w, other_w, back, upstream, sent, grad_out, send, sems):
    tokens = upstream.shape[0]
    upper = on_core(1)
    clear(send, send.shape[0])

    def token(t, carry):
        total = upstream[t].astype(F32)
        for k in range(2):
            total = total + back[slots[1, 2 * t + k]].astype(F32)
        rounded = total.astype(BF16)
        grad_out[t] = rounded
        g = rounded.astype(F32)
        for k in range(2):
            p = 2 * t + k
            weight = jnp.where(upper, other_w[p], own_w[p])
            send[slots[0, p]] = (weight * g).astype(BF16)
        return carry

    lax.fori_loop(0, tokens, token, 0, unroll=4)
    fetch(send, sent, sems.at[0]).wait()


def finish_kernel(slots, back, upstream, keep, away, low, up):
    tokens, depth = upstream.shape[0], upstream.shape[1]
    upper = on_core(1)

    def token(t, carry):
        at = pl.ds(pl.multiple_of(t * depth, depth), depth)
        g = upstream[t].astype(F32)
        up[at, :] = g
        total = g
        for k in range(2):
            total = total + back[slots[0, 2 * t + k]].astype(F32)
        low[at, :] = total
        return carry

    lax.fori_loop(0, tokens, token, 0, unroll=4)
    for j in range(depth):
        columns = slice(j * LANES, (j + 1) * LANES)
        high = up[pl.ds(j, tokens, stride=depth), :]
        down = low[pl.ds(j, tokens, stride=depth), :]
        keep[:, columns] = jnp.where(upper, high, down).astype(BF16)
        away[:, columns] = jnp.where(upper, down, high).astype(BF16)


def turn_kernel(turn, gate, up, down, *refs):
    gate_up_t, down_t, a, b, c, turned, turned_down, sems = refs[-8:]
    hidden, width = down.shape
    step = 256

    def work():
        copies = [
            fetch(gate, a, sems.at[0]), fetch(up, b, sems.at[1]), fetch(down, c, sems.at[2])
        ]
        for n, block in enumerate((a, b)):
            copies[n].wait()
            for i in range(0, width, step):
                turned[n * hidden : (n + 1) * hidden, i : i + step] = block[i : i + step, :].T
        first = fetch(turned, gate_up_t, sems.at[3])
        copies[2].wait()
        for i in range(0, width, step):
            turned_down[i : i + step, :] = c[:, i : i + step].T
        fetch(turned_down, down_t, sems.at[4]).wait()
        first.wait()

    if turn is None:
        work()
    else:
        pl.when(on_core(turn))(work)


def untile(block, tiles, rows, depth):
    count, lanes = rows.shape[0], LANES
    tiles[...] = block[...].astype(F32).reshape(count * depth, lanes)
    tiles_to_rows(tiles, rows, count, depth)


def forward_parts(rows, gate, up):
    hidden_gate = jnp.dot(rows[...], gate[...], preferred_element_type=F32)
    hidden_up = jnp.dot(rows[...], up[...], preferred_element_type=F32)
    sigma = 1.0 / (1.0 + jnp.exp(-hidden_gate))
    act = hidden_gate * sigma
    dact = sigma * (1.0 + hidden_gate * (1.0 - sigma))
    return act, hidden_up * dact, (act * hidden_up).astype(BF16)


def backward_parts(act, slope, dy_rows, down_t, matrices, gate_up_t, tiles, send, sent, sem):
    count, depth, lanes = send.shape
    grad_act = jnp.dot(dy_rows[...], down_t[...], preferred_element_type=F32)
    both = jnp.concatenate(
        [(grad_act * slope).astype(BF16), (grad_act * act).astype(BF16)], axis=1
    )
    matrices.wait()
    dx = jnp.dot(both, gate_up_t[...], preferred_element_type=F32)
    rows_to_tiles(dx, tiles, count, depth)
    pieces, copies = 4, []
    part = count // pieces
    for n in range(pieces):
        rows = tiles[n * part * depth : (n + 1) * part * depth, :]
        send[n * part : (n + 1) * part] = rows.reshape(part, depth, lanes).astype(BF16)
        here = pl.ds(n * part, part)
        copies.append(fetch(send.at[here], sent.at[here], sem.at[n]))
    return copies


def upper_kernel(
    arrived, own_gate, other_gate, own_up, other_up, own_dt, other_dt, own_gut, other_gut,
    sent, dy_out, act_out,
    x, dy, gate, up, down_t, gate_up_t, tiles, x_rows, dy_rows, activ, send, sems,
):
    mine = on_core(1)
    depth = send.shape[1]
    x_copy = fetch(arrived.at[:, :CAP], x, sems.at[0])
    gate_copy = fetch_one_of(mine, own_gate, other_gate, gate, sems.at[1])
    up_copy = fetch_one_of(mine, own_up, other_up, up, sems.at[2])
    dy_copy = fetch(arrived.at[:, CAP : 2 * CAP], dy, sems.at[3])
    down_copy = fetch_one_of(mine, own_dt, other_dt, down_t, sems.at[4])
    back_copy = fetch_one_of(mine, own_gut, other_gut, gate_up_t, sems.at[5])
    x_copy.wait()
    untile(x, tiles, x_rows, depth)
    gate_copy.wait()
    up_copy.wait()
    act, slope, rounded = forward_parts(x_rows, gate, up)
    activ[...] = rounded
    dy_copy.wait()
    untile(dy, tiles, dy_rows, depth)
    saves = [fetch(activ, act_out, sems.at[6]), fetch(dy_rows, dy_out, sems.at[7])]
    down_copy.wait()
    saves += backward_parts(
        act, slope, dy_rows, down_t, back_copy, gate_up_t, tiles, send, sent, sems.at[pl.ds(8, 4)]
    )
    for copy in saves:
        copy.wait()


def forward_kernel(
    arrived, own_gate, other_gate, own_up, other_up, act_out, slope_out, activ_out,
    x, gate, up, tiles, x_rows, sems,
):
    mine = on_core(0)
    depth = arrived.shape[2]
    x_copy = fetch(arrived.at[:, 2 * CAP :], x, sems.at[0])
    gate_copy = fetch_one_of(mine, own_gate, other_gate, gate, sems.at[1])
    up_copy = fetch_one_of(mine, own_up, other_up, up, sems.at[2])
    x_copy.wait()
    untile(x, tiles, x_rows, depth)
    gate_copy.wait()
    up_copy.wait()
    act, slope, rounded = forward_parts(x_rows, gate, up)
    act_out[...] = act
    slope_out[...] = slope
    activ_out[...] = rounded


def lower_kernel(
    dy, act, slope, own_dt, other_dt, own_gut, other_gut, sent, dy_out,
    down_t, gate_up_t, tiles, dy_rows, send, sems,
):
    mine = on_core(0)
    down_copy = fetch_one_of(mine, own_dt, other_dt, down_t, sems.at[0])
    back_copy = fetch_one_of(mine, own_gut, other_gut, gate_up_t, sems.at[1])
    untile(dy, tiles, dy_rows, send.shape[1])
    save = fetch(dy_rows, dy_out, sems.at[2])
    down_copy.wait()
    saves = backward_parts(
        act[...], slope[...], dy_rows, down_t, back_copy, gate_up_t, tiles, send, sent,
        sems.at[pl.ds(3, 4)],
    )
    for copy in saves:
        copy.wait()
    save.wait()


def call(kernel, args, in_specs, out_shape, out_specs, scratch, flops, moved, aliases={}):
    return pl.pallas_call(
        kernel,
        in_specs=in_specs,
        out_shape=out_shape,
        out_specs=out_specs,
        scratch_shapes=scratch,
        input_output_aliases=aliases,
        compiler_params=pltpu.CompilerParams(vmem_limit_bytes=63 * 1024 * 1024),
        cost_estimate=pl.CostEstimate(flops=flops, bytes_accessed=moved, transcendentals=0),
    )(*args)


def swapped(block):
    return lax.ppermute(block, "segment", [(0, 1), (1, 0)])


def exchanged(block):
    return lax.all_to_all(block, "expert", split_axis=0, concat_axis=0, tiled=True)


def shape(dims, kind=BF16):
    return jax.ShapeDtypeStruct(dims, kind)


def shards(saved_input, out_grad, expert_ids, router_weights, w_gate, w_up, w_down, eigenbasis):
    experts = lax.axis_size("expert")
    segment = lax.axis_index("segment")
    upper = segment == 1
    micros, tokens, width = saved_input.shape[1:]
    hidden = w_gate.shape[-1]
    depth = width // LANES
    count = experts * CAP
    gate, up, down, basis = w_gate[0, 0], w_up[0, 0], w_down[0, 0], eigenbasis[0, 0]

    ids = expert_ids[0].reshape(micros, tokens * 2)
    weights = router_weights[0].reshape(micros, tokens * 2)
    mine = functools.partial(lax.dynamic_index_in_dim, index=segment, axis=0, keepdims=False)
    theirs = functools.partial(lax.dynamic_index_in_dim, index=1 - segment, axis=0, keepdims=False)
    own_x, other_x = mine(saved_input[0]), swapped(theirs(saved_input[0]))
    own_ids, other_ids = mine(ids), swapped(theirs(ids))
    own_w, other_w = mine(weights), swapped(theirs(weights))
    grad = mine(out_grad)

    matrix = pltpu.VMEM((width, hidden), BF16)
    turned_shapes = (shape((2 * hidden, width)), shape((width, hidden)))
    turn_scratch = [
        matrix, matrix, pltpu.VMEM((hidden, width), BF16), pltpu.VMEM((2 * hidden, width), BF16),
        matrix, pltpu.SemaphoreType.DMA((5,)),
    ]

    def turned(turn, matrices, made=()):
        return call(
            functools.partial(turn_kernel, turn),
            (*matrices, *made),
            [HBM] * (3 + len(made)),
            turned_shapes,
            (HBM,) * 2,
            turn_scratch,
            1_000_000,
            9_000_000,
            {3: 0, 4: 1} if made else {},
        )

    early_gut, early_dt = turned(0, (gate, up, down))

    tile_rows = tokens * depth
    send, slots, grad_tiles = call(
        dispatch_kernel,
        (own_ids, other_ids, own_w, other_w, own_x, other_x, grad, early_dt),
        [SMEM] * 4 + [VMEM] * 3 + [HBM],
        (
            shape((experts, 3 * CAP, depth, LANES)),
            shape((2, tokens * 2), jnp.int32),
            shape((tokens, depth, LANES)),
        ),
        (HBM, SMEM, VMEM),
        [pltpu.VMEM((experts, 3 * CAP, depth, LANES), BF16)]
        + [pltpu.VMEM((tile_rows, LANES), F32)] * 3
        + [pltpu.SMEM((2, experts), jnp.int32), pltpu.SemaphoreType.DMA((2,))],
        1_000_000,
        5_000_000,
    )
    arrived = exchanged(send)

    own_gut, own_dt = turned(1, (gate, up, down), (early_gut, early_dt))
    other_gate, other_up, other_down = swapped(gate), swapped(up), swapped(down)
    other_basis = swapped(basis)
    other_gut, other_dt = turned(None, (other_gate, other_up, other_down))

    tiles = pltpu.VMEM((count * depth, LANES), F32)
    rows = pltpu.VMEM((count, width), BF16)
    part = pltpu.VMEM((experts, CAP, depth, LANES), BF16)
    flat = (count, depth, LANES)
    flat_scratch = pltpu.VMEM(flat, BF16)
    mat = 2 * count * width * hidden
    back_send, dy_rows1, activ1 = call(
        upper_kernel,
        (arrived, gate, other_gate, up, other_up, own_dt, other_dt, own_gut, other_gut),
        [HBM] * 9,
        (shape(flat), shape((count, width)), shape((count, hidden))),
        (HBM,) * 3,
        [
            part, part, matrix, matrix, matrix, pltpu.VMEM((2 * hidden, width), BF16), tiles,
            rows, rows, pltpu.VMEM((count, hidden), BF16), flat_scratch,
            pltpu.SemaphoreType.DMA((12,)),
        ],
        5 * mat,
        9_000_000,
    )

    def returned(block):
        return exchanged(block.reshape(experts, CAP, depth, LANES)).reshape(flat)

    back = returned(back_send)
    act0, slope0, activ0 = call(
        forward_kernel,
        (arrived, gate, other_gate, up, other_up),
        [HBM] * 5,
        (shape((count, hidden), F32), shape((count, hidden), F32), shape((count, hidden))),
        (VMEM,) * 3,
        [part, matrix, matrix, tiles, rows, pltpu.SemaphoreType.DMA((3,))],
        2 * mat,
        5_000_000,
    )
    basis1 = jnp.where(upper, basis, other_basis)
    basis0 = jnp.where(upper, other_basis, basis)
    rotated1 = jnp.dot(activ1, basis1, preferred_element_type=F32).astype(BF16)
    rotated0 = jnp.dot(activ0, basis0, preferred_element_type=F32).astype(BF16)

    dy_send, grad1 = call(
        relay_kernel,
        (slots, own_w, other_w, back, grad_tiles),
        [SMEM] * 3 + [VMEM] * 2,
        (shape(flat), shape((tokens, depth, LANES))),
        (HBM, VMEM),
        [flat_scratch, pltpu.SemaphoreType.DMA((1,))],
        1_000_000,
        3_000_000,
    )
    dy = returned(dy_send)
    back_send0, dy_rows0 = call(
        lower_kernel,
        (dy, act0, slope0, own_dt, other_dt, own_gut, other_gut),
        [VMEM] * 3 + [HBM] * 4,
        (shape(flat), shape((count, width))),
        (HBM,) * 2,
        [
            matrix, pltpu.VMEM((2 * hidden, width), BF16), tiles, rows, flat_scratch,
            pltpu.SemaphoreType.DMA((7,)),
        ],
        3 * mat,
        8_000_000,
    )
    back0 = returned(back_send0)

    all_rotated = jnp.concatenate(
        [
            jnp.where(upper, rotated1, rotated0),
            swapped(jnp.where(upper, rotated0, rotated1)),
        ],
        axis=0,
    )
    all_dy = jnp.concatenate(
        [
            jnp.where(upper, dy_rows1, dy_rows0),
            swapped(jnp.where(upper, dy_rows0, dy_rows1)),
        ],
        axis=0,
    )
    rot_sq = (all_rotated.astype(F32) ** 2).astype(BF16)
    dy_sq = (all_dy.astype(F32) ** 2).astype(BF16)
    over_rows = (((0,), (0,)), ((), ()))
    grad_sum = lax.dot_general(all_rotated, all_dy, over_rows, preferred_element_type=F32)
    scale_sum = lax.dot_general(rot_sq, dy_sq, over_rows, preferred_element_type=F32)
    rotated_grad = (grad_sum * (1.0 / micros)).astype(BF16)
    ekfac_scales = scale_sum * (1.0 / micros)
    back0, rotated_grad, ekfac_scales = lax.optimization_barrier(
        (back0, rotated_grad, ekfac_scales)
    )

    keep, away = call(
        finish_kernel,
        (slots, back0, grad1),
        [SMEM] + [VMEM] * 2,
        (shape((tokens, width)), shape((tokens, width))),
        (VMEM,) * 2,
        [pltpu.VMEM((tile_rows, LANES), F32)] * 2,
        1_000_000,
        2_000_000,
    )
    came = swapped(away)
    grads = jnp.stack([jnp.where(upper, came, keep), jnp.where(upper, keep, came)])
    return (grads[None], rotated_grad[None, None], ekfac_scales[None, None])


def solution(mesh):
    in_specs = (
        P("segment", None, "expert", None),
        P(None, "expert", None),
        P("segment", None, "expert", None),
        P("segment", None, "expert", None),
        P("segment", "expert", None, None),
        P("segment", "expert", None, None),
        P("segment", "expert", None, None),
        P("segment", "expert", None, None),
    )
    out_specs = (
        P("segment", None, "expert", None),
        P("segment", "expert", None, None),
        P("segment", "expert", None, None),
    )
    return jax.shard_map(shards, mesh=mesh, in_specs=in_specs, out_specs=out_specs, check_vma=False)
```

```python
import functools
import jax
import jax.numpy as jnp
from jax import lax
from jax.experimental import pallas as pl
from jax.experimental.pallas import tpu as pltpu
from jax.sharding import PartitionSpec as P

LANES = 128
CAP = 2
F32 = jnp.float32
BF16 = jnp.bfloat16
SMEM = pl.BlockSpec(memory_space=pltpu.SMEM)
VMEM = pl.BlockSpec(memory_space=pltpu.VMEM)
HBM = pl.BlockSpec(memory_space=pltpu.HBM)


def rows_to_tiles(rows, tiles, count, depth):
    for j in range(depth):
        tiles[pl.ds(j, count, stride=depth), :] = rows[:, j * LANES : (j + 1) * LANES]


def tiles_to_rows(tiles, rows, count, depth):
    for j in range(depth):
        rows[:, j * LANES : (j + 1) * LANES] = tiles[pl.ds(j, count, stride=depth), :].astype(
            rows.dtype
        )


def clear(send, experts):
    zero = jnp.zeros(send.shape[1:], send.dtype)

    def one(e, carry):
        send[e] = zero
        return carry

    lax.fori_loop(0, experts, one, 0, unroll=8)


def on_core(which):
    return lax.axis_index("segment") == which


def fetch(source, target, sem):
    copy = pltpu.make_async_copy(source, target, sem)
    copy.start()
    return copy


def fetch_one_of(first, own, other, target, sem):
    @pl.when(first)
    def _():
        pltpu.make_async_copy(own, target, sem).start()

    @pl.when(jnp.logical_not(first))
    def _():
        pltpu.make_async_copy(other, target, sem).start()

    return pltpu.make_async_copy(own, target, sem)


def dispatch_kernel(core, own_ids, other_ids, own_w, other_w, own_x, other_x, grads, *refs):
    sent, slots_out, tiles_out = refs[-14:-11]
    send, slots, grad_tiles, own, other, grad, x_upper, x_lower, g_tiles, counts, sems = refs[-11:]
    tokens, width = grad.shape
    depth = width // LANES
    experts = send.shape[0]
    upper = core == 1

    def work():
        copies = [
            fetch(own_x.at[core], own, sems.at[0]),
            fetch(other_x, other, sems.at[1]),
            fetch(grads.at[core], grad, sems.at[2]),
        ]
        first_ids, second_ids = (own_ids, other_ids) if upper else (other_ids, own_ids)
        weights = own_w if upper else other_w
        clear(send, experts)

        def reset(e, carry):
            counts[0, e] = 0
            counts[1, e] = 0
            return carry

        lax.fori_loop(0, experts, reset, 0, unroll=8)
        for copy in copies:
            copy.wait()
        first_x, second_x = (own, other) if upper else (other, own)
        rows_to_tiles(first_x[...].astype(F32), x_upper, tokens, depth)
        rows_to_tiles(second_x[...].astype(F32), x_lower, tokens, depth)
        rows_to_tiles(grad[...].astype(F32), g_tiles, tokens, depth)

        def first(t, carry):
            at = pl.ds(pl.multiple_of(t * depth, depth), depth)
            row = x_upper[at, :].astype(BF16)
            g = g_tiles[at, :]
            grad_tiles[t] = g.astype(BF16)
            for k in range(2):
                p = 2 * t + k
                e = first_ids[core, p]
                c = jnp.minimum(counts[0, e], CAP - 1)
                counts[0, e] = c + 1
                slots[1, p] = e * CAP + c
                send[e, c] = row
                send[e, CAP + c] = (weights[core, p] * g).astype(BF16)
            return carry

        lax.fori_loop(0, tokens, first, 0, unroll=2)
        saves = [
            fetch(send.at[:, : 2 * CAP], sent.at[:, : 2 * CAP], sems.at[3]),
            fetch(grad_tiles, tiles_out, sems.at[4]),
        ]

        def second(t, carry):
            at = pl.ds(pl.multiple_of(t * depth, depth), depth)
            row = x_lower[at, :].astype(BF16)
            for k in range(2):
                p = 2 * t + k
                e = second_ids[core, p]
                c = jnp.minimum(counts[1, e], CAP - 1)
                counts[1, e] = c + 1
                slots[0, p] = e * CAP + c
                send[e, 2 * CAP + c] = row
            return carry

        lax.fori_loop(0, tokens, second, 0, unroll=2)
        saves.append(fetch(send.at[:, 2 * CAP :], sent.at[:, 2 * CAP :], sems.at[5]))
        saves.append(fetch(slots, slots_out, sems.at[6]))
        for copy in saves:
            copy.wait()

    pl.when(on_core(core))(work)


def relay_kernel(slots, own_w, other_w, back, upstream, sent, grad_out, send, sems):
    tokens = upstream.shape[0]
    upper = on_core(1)
    clear(send, send.shape[0])

    def token(t, carry):
        total = upstream[t].astype(F32)
        for k in range(2):
            total = total + back[slots[1, 2 * t + k]].astype(F32)
        rounded = total.astype(BF16)
        grad_out[t] = rounded
        g = rounded.astype(F32)
        for k in range(2):
            p = 2 * t + k
            weight = jnp.where(upper, other_w[1, p], own_w[0, p])
            send[slots[0, p]] = (weight * g).astype(BF16)
        return carry

    lax.fori_loop(0, tokens, token, 0, unroll=4)
    fetch(send, sent, sems.at[0]).wait()


def finish_kernel(slots, back, upstream, keep, away, low, up):
    tokens, depth = upstream.shape[0], upstream.shape[1]
    upper = on_core(1)

    def token(t, carry):
        at = pl.ds(pl.multiple_of(t * depth, depth), depth)
        g = upstream[t].astype(F32)
        up[at, :] = g
        total = g
        for k in range(2):
            total = total + back[slots[0, 2 * t + k]].astype(F32)
        low[at, :] = total
        return carry

    lax.fori_loop(0, tokens, token, 0, unroll=4)
    for j in range(depth):
        columns = slice(j * LANES, (j + 1) * LANES)
        high = up[pl.ds(j, tokens, stride=depth), :]
        down = low[pl.ds(j, tokens, stride=depth), :]
        keep[:, columns] = jnp.where(upper, high, down).astype(BF16)
        away[:, columns] = jnp.where(upper, down, high).astype(BF16)


def turn_kernel(core, *refs):
    outs, (a, b, c, turned, turned_down, sems) = refs[-10:-6], refs[-6:]
    hidden, width = refs[2].shape
    step = 256

    def work():
        saves = []
        for layer in range(2):
            copies = [
                fetch(source, target, sems.at[layer, n])
                for n, (source, target) in enumerate(
                    zip(refs[3 * layer : 3 * layer + 3], (a.at[layer], b.at[layer], c.at[layer]))
                )
            ]
            saves.append(copies)
        for layer, copies in enumerate(saves):
            gate_up_t, down_t = outs[2 * layer], outs[2 * layer + 1]
            for n, block in enumerate((a, b)):
                copies[n].wait()
                for i in range(0, width, step):
                    turned[layer, n * hidden : (n + 1) * hidden, i : i + step] = block[
                        layer, i : i + step, :
                    ].T
            copies.append(fetch(turned.at[layer], gate_up_t, sems.at[layer, 3]))
            copies[2].wait()
            for i in range(0, width, step):
                turned_down[layer, i : i + step, :] = c[layer, :, i : i + step].T
            copies.append(fetch(turned_down.at[layer], down_t, sems.at[layer, 4]))
        for copies in saves:
            copies[3].wait()
            copies[4].wait()

    pl.when(on_core(core))(work)


def untile(block, tiles, rows, depth):
    count, lanes = rows.shape[0], LANES
    tiles[...] = block[...].astype(F32).reshape(count * depth, lanes)
    tiles_to_rows(tiles, rows, count, depth)


def forward_parts(rows, gate, up):
    hidden_gate = jnp.dot(rows[...], gate[...], preferred_element_type=F32)
    hidden_up = jnp.dot(rows[...], up[...], preferred_element_type=F32)
    sigma = 1.0 / (1.0 + jnp.exp(-hidden_gate))
    act = hidden_gate * sigma
    dact = sigma * (1.0 + hidden_gate * (1.0 - sigma))
    return act, hidden_up * dact, (act * hidden_up).astype(BF16)


def backward_parts(act, slope, dy_rows, down_t, matrices, gate_up_t, tiles, send, sent, sem):
    count, depth, lanes = send.shape
    grad_act = jnp.dot(dy_rows[...], down_t[...], preferred_element_type=F32)
    both = jnp.concatenate(
        [(grad_act * slope).astype(BF16), (grad_act * act).astype(BF16)], axis=1
    )
    matrices.wait()
    dx = jnp.dot(both, gate_up_t[...], preferred_element_type=F32)
    rows_to_tiles(dx, tiles, count, depth)
    pieces, copies = 4, []
    part = count // pieces
    for n in range(pieces):
        rows = tiles[n * part * depth : (n + 1) * part * depth, :]
        send[n * part : (n + 1) * part] = rows.reshape(part, depth, lanes).astype(BF16)
        here = pl.ds(n * part, part)
        copies.append(fetch(send.at[here], sent.at[here], sem.at[n]))
    return copies


def upper_kernel(
    arrived, own_gate, other_gate, own_up, other_up, turned_down, turned,
    sent, dy_out, act_out,
    x, dy, gate, up, down_t, gate_up_t, tiles, x_rows, dy_rows, activ, send, sems,
):
    mine = on_core(1)
    depth = send.shape[1]
    x_copy = fetch(arrived.at[:, :CAP], x, sems.at[0])
    gate_copy = fetch_one_of(mine, own_gate, other_gate, gate, sems.at[1])
    up_copy = fetch_one_of(mine, own_up, other_up, up, sems.at[2])
    dy_copy = fetch(arrived.at[:, CAP : 2 * CAP], dy, sems.at[3])
    down_copy = fetch(turned_down, down_t, sems.at[4])
    back_copy = fetch(turned, gate_up_t, sems.at[5])
    x_copy.wait()
    untile(x, tiles, x_rows, depth)
    gate_copy.wait()
    up_copy.wait()
    act, slope, rounded = forward_parts(x_rows, gate, up)
    activ[...] = rounded
    dy_copy.wait()
    untile(dy, tiles, dy_rows, depth)
    saves = [fetch(activ, act_out, sems.at[6]), fetch(dy_rows, dy_out, sems.at[7])]
    down_copy.wait()
    saves += backward_parts(
        act, slope, dy_rows, down_t, back_copy, gate_up_t, tiles, send, sent, sems.at[pl.ds(8, 4)]
    )
    for copy in saves:
        copy.wait()


def forward_kernel(
    arrived, own_gate, other_gate, own_up, other_up, act_out, slope_out, activ_out,
    x, gate, up, tiles, x_rows, sems,
):
    mine = on_core(0)
    depth = arrived.shape[2]
    x_copy = fetch(arrived.at[:, 2 * CAP :], x, sems.at[0])
    gate_copy = fetch_one_of(mine, own_gate, other_gate, gate, sems.at[1])
    up_copy = fetch_one_of(mine, own_up, other_up, up, sems.at[2])
    x_copy.wait()
    untile(x, tiles, x_rows, depth)
    gate_copy.wait()
    up_copy.wait()
    act, slope, rounded = forward_parts(x_rows, gate, up)
    act_out[...] = act
    slope_out[...] = slope
    activ_out[...] = rounded


def lower_kernel(
    dy, act, slope, turned_down, turned, sent, dy_out,
    down_t, gate_up_t, tiles, dy_rows, send, sems,
):
    down_copy = fetch(turned_down, down_t, sems.at[0])
    back_copy = fetch(turned, gate_up_t, sems.at[1])
    untile(dy, tiles, dy_rows, send.shape[1])
    save = fetch(dy_rows, dy_out, sems.at[2])
    down_copy.wait()
    saves = backward_parts(
        act[...], slope[...], dy_rows, down_t, back_copy, gate_up_t, tiles, send, sent,
        sems.at[pl.ds(3, 4)],
    )
    for copy in saves:
        copy.wait()
    save.wait()


def call(kernel, args, in_specs, out_shape, out_specs, scratch, flops, moved, aliases={}):
    return pl.pallas_call(
        kernel,
        in_specs=in_specs,
        out_shape=out_shape,
        out_specs=out_specs,
        scratch_shapes=scratch,
        input_output_aliases=aliases,
        compiler_params=pltpu.CompilerParams(vmem_limit_bytes=63 * 1024 * 1024),
        cost_estimate=pl.CostEstimate(flops=flops, bytes_accessed=moved, transcendentals=0),
    )(*args)


def swapped(block):
    return lax.ppermute(block, "segment", [(0, 1), (1, 0)])


def exchanged(block):
    return lax.all_to_all(block, "expert", split_axis=0, concat_axis=0, tiled=True)


def shape(dims, kind=BF16):
    return jax.ShapeDtypeStruct(dims, kind)


def shards(saved_input, out_grad, expert_ids, router_weights, w_gate, w_up, w_down, eigenbasis):
    experts = lax.axis_size("expert")
    segment = lax.axis_index("segment")
    upper = segment == 1
    micros, tokens, width = saved_input.shape[1:]
    hidden = w_gate.shape[-1]
    depth = width // LANES
    count = experts * CAP
    gate, up, down, basis = w_gate[0, 0], w_up[0, 0], w_down[0, 0], eigenbasis[0, 0]

    theirs = lax.dynamic_index_in_dim(saved_input[0], 1 - segment, 0, keepdims=False)
    other_x = swapped(theirs)
    own_ids = expert_ids[0].reshape(micros, tokens * 2)
    own_w = router_weights[0].reshape(micros, tokens * 2)
    other_ids, other_w = swapped(own_ids), swapped(own_w)

    tile_rows = tokens * depth
    matrix = pltpu.VMEM((width, hidden), BF16)
    pair = pltpu.VMEM((2, width, hidden), BF16)
    pair_t = pltpu.VMEM((2, 2 * hidden, width), BF16)
    row_block = pltpu.VMEM((tokens, width), BF16)

    def dispatched(core, after, made=()):
        inputs = (own_ids, other_ids, own_w, other_w, saved_input[0], other_x, out_grad)
        return call(
            functools.partial(dispatch_kernel, core),
            (*inputs, *after, *made),
            [SMEM] * 4 + [HBM] * (3 + len(after) + len(made)),
            (
                shape((experts, 3 * CAP, depth, LANES)),
                shape((2, tokens * 2), jnp.int32),
                shape((tokens, depth, LANES)),
            ),
            (HBM,) * 3,
            [
                pltpu.VMEM((experts, 3 * CAP, depth, LANES), BF16),
                pltpu.SMEM((2, tokens * 2), jnp.int32),
                pltpu.VMEM((tokens, depth, LANES), BF16),
            ]
            + [row_block] * 3
            + [pltpu.VMEM((tile_rows, LANES), F32)] * 3
            + [pltpu.SMEM((2, experts), jnp.int32), pltpu.SemaphoreType.DMA((7,))],
            1_000_000,
            5_000_000,
            {len(inputs) + len(after) + n: n for n in range(len(made))},
        )

    def turned(core, matrices, after, made=()):
        return call(
            functools.partial(turn_kernel, core),
            (*matrices, *after, *made),
            [HBM] * (6 + len(after) + len(made)),
            (shape((2 * hidden, width)), shape((width, hidden))) * 2,
            (HBM,) * 4,
            [
                pair, pair, pltpu.VMEM((2, hidden, width), BF16), pair_t, pair,
                pltpu.SemaphoreType.DMA((2, 5)),
            ],
            1_000_000,
            18_000_000,
            {6 + len(after) + n: n for n in range(len(made))},
        )

    def moved(block, source):
        return lax.ppermute(block, "segment", [(source, 1 - source)])

    first_sent = dispatched(1, ())
    layer1 = tuple(moved(block, 1) for block in (gate, up, down))
    early = turned(0, (*layer1, gate, up, down), first_sent[2:])
    send, slots, grad_tiles = dispatched(0, early[:1], first_sent)
    arrived = exchanged(send)

    layer0 = tuple(moved(block, 0) for block in (gate, up, down))
    other_basis = swapped(basis)
    gut1, dt1, gut0, dt0 = turned(1, (gate, up, down, *layer0), (), early)

    tiles = pltpu.VMEM((count * depth, LANES), F32)
    rows = pltpu.VMEM((count, width), BF16)
    part = pltpu.VMEM((experts, CAP, depth, LANES), BF16)
    flat = (count, depth, LANES)
    flat_scratch = pltpu.VMEM(flat, BF16)
    mat = 2 * count * width * hidden
    back_send, dy_rows1, activ1 = call(
        upper_kernel,
        (arrived, gate, layer1[0], up, layer1[1], dt1, gut1),
        [HBM] * 7,
        (shape(flat), shape((count, width)), shape((count, hidden))),
        (HBM,) * 3,
        [
            part, part, matrix, matrix, matrix, pltpu.VMEM((2 * hidden, width), BF16), tiles,
            rows, rows, pltpu.VMEM((count, hidden), BF16), flat_scratch,
            pltpu.SemaphoreType.DMA((12,)),
        ],
        5 * mat,
        9_000_000,
    )

    def returned(block):
        return exchanged(block.reshape(experts, CAP, depth, LANES)).reshape(flat)

    back = returned(back_send)
    act0, slope0, activ0 = call(
        forward_kernel,
        (arrived, gate, layer0[0], up, layer0[1]),
        [HBM] * 5,
        (shape((count, hidden), F32), shape((count, hidden), F32), shape((count, hidden))),
        (VMEM,) * 3,
        [part, matrix, matrix, tiles, rows, pltpu.SemaphoreType.DMA((3,))],
        2 * mat,
        5_000_000,
    )
    basis1 = jnp.where(upper, basis, other_basis)
    basis0 = jnp.where(upper, other_basis, basis)
    rotated1 = jnp.dot(activ1, basis1, preferred_element_type=F32).astype(BF16)
    rotated0 = jnp.dot(activ0, basis0, preferred_element_type=F32).astype(BF16)

    dy_send, grad1 = call(
        relay_kernel,
        (slots, own_w, other_w, back, grad_tiles),
        [SMEM] * 3 + [VMEM] * 2,
        (shape(flat), shape((tokens, depth, LANES))),
        (HBM, VMEM),
        [flat_scratch, pltpu.SemaphoreType.DMA((1,))],
        1_000_000,
        3_000_000,
    )
    dy = returned(dy_send)
    back_send0, dy_rows0 = call(
        lower_kernel,
        (dy, act0, slope0, dt0, gut0),
        [VMEM] * 3 + [HBM] * 2,
        (shape(flat), shape((count, width))),
        (HBM,) * 2,
        [
            matrix, pltpu.VMEM((2 * hidden, width), BF16), tiles, rows, flat_scratch,
            pltpu.SemaphoreType.DMA((7,)),
        ],
        3 * mat,
        8_000_000,
    )
    back0 = returned(back_send0)

    all_rotated = jnp.concatenate(
        [
            jnp.where(upper, rotated1, rotated0),
            swapped(jnp.where(upper, rotated0, rotated1)),
        ],
        axis=0,
    )
    all_dy = jnp.concatenate(
        [
            jnp.where(upper, dy_rows1, dy_rows0),
            swapped(jnp.where(upper, dy_rows0, dy_rows1)),
        ],
        axis=0,
    )
    rot_sq = (all_rotated.astype(F32) ** 2).astype(BF16)
    dy_sq = (all_dy.astype(F32) ** 2).astype(BF16)
    over_rows = (((0,), (0,)), ((), ()))
    grad_sum = lax.dot_general(all_rotated, all_dy, over_rows, preferred_element_type=F32)
    scale_sum = lax.dot_general(rot_sq, dy_sq, over_rows, preferred_element_type=F32)
    rotated_grad = (grad_sum * (1.0 / micros)).astype(BF16)
    ekfac_scales = scale_sum * (1.0 / micros)
    back0, rotated_grad, ekfac_scales = lax.optimization_barrier(
        (back0, rotated_grad, ekfac_scales)
    )

    keep, away = call(
        finish_kernel,
        (slots, back0, grad1),
        [SMEM] + [VMEM] * 2,
        (shape((tokens, width)), shape((tokens, width))),
        (VMEM,) * 2,
        [pltpu.VMEM((tile_rows, LANES), F32)] * 2,
        1_000_000,
        2_000_000,
    )
    came = swapped(away)
    grads = jnp.stack([jnp.where(upper, came, keep), jnp.where(upper, keep, came)])
    return (grads[None], rotated_grad[None, None], ekfac_scales[None, None])


def solution(mesh):
    in_specs = (
        P("segment", None, "expert", None),
        P(None, "expert", None),
        P("segment", None, "expert", None),
        P("segment", None, "expert", None),
        P("segment", "expert", None, None),
        P("segment", "expert", None, None),
        P("segment", "expert", None, None),
        P("segment", "expert", None, None),
    )
    out_specs = (
        P("segment", None, "expert", None),
        P("segment", "expert", None, None),
        P("segment", "expert", None, None),
    )
    return jax.shard_map(shards, mesh=mesh, in_specs=in_specs, out_specs=out_specs, check_vma=False)
```

```python
import functools
import jax
import jax.numpy as jnp
import numpy as np
from jax import lax
from jax.experimental import pallas as pl
from jax.experimental.pallas import tpu as pltpu
from jax.sharding import PartitionSpec as P

LANES = 128
CAP = 2
F32 = jnp.float32
BF16 = jnp.bfloat16
SMEM = pl.BlockSpec(memory_space=pltpu.SMEM)
VMEM = pl.BlockSpec(memory_space=pltpu.VMEM)
HBM = pl.BlockSpec(memory_space=pltpu.HBM)


def rows_to_tiles(rows, tiles, count, depth):
    for j in range(depth):
        tiles[pl.ds(j, count, stride=depth), :] = rows[:, j * LANES : (j + 1) * LANES]


def tile_columns(tiles, first, number, count, depth):
    return jnp.concatenate(
        [tiles[pl.ds(j, count, stride=depth), :] for j in range(first, first + number)], axis=1
    ).astype(BF16)


def clear(send, experts):
    zero = jnp.zeros(send.shape[1:], send.dtype)

    def one(e, carry):
        send[e] = zero
        return carry

    lax.fori_loop(0, experts, one, 0, unroll=8)


def on_core(which):
    return lax.axis_index("segment") == which


def fetch(source, target, sem):
    copy = pltpu.make_async_copy(source, target, sem)
    copy.start()
    return copy


def fetch_one_of(first, own, other, target, sem):
    @pl.when(first)
    def _():
        pltpu.make_async_copy(own, target, sem).start()

    @pl.when(jnp.logical_not(first))
    def _():
        pltpu.make_async_copy(other, target, sem).start()

    return pltpu.make_async_copy(own, target, sem)


def slot_reader(own_slots, other_slots):
    segment = lax.axis_index("segment")

    def slot(layer, k, t):
        mine, theirs = own_slots[segment, k, t], other_slots[segment, k, t]
        return jnp.where(segment == layer, mine, theirs)

    return slot


def dispatch_kernel(
    own_slots, other_slots, own_w, other_w, own_x, other_x, grads, after, sent, tiles_out,
    send, grad_tiles, own, other, grad, x_upper, x_lower, g_tiles, sems,
):
    tokens, width = grad.shape
    depth = width // LANES
    segment = lax.axis_index("segment")
    upper = segment == 1
    slot = slot_reader(own_slots, other_slots)
    copies = [
        fetch(own_x.at[segment], own, sems.at[0]),
        fetch(other_x, other, sems.at[1]),
        fetch(grads.at[segment], grad, sems.at[2]),
    ]
    clear(send, send.shape[0])
    for copy in copies:
        copy.wait()
    mine, theirs = own[...].astype(F32), other[...].astype(F32)
    rows_to_tiles(jnp.where(upper, mine, theirs), x_upper, tokens, depth)
    saves = []

    def part(n):
        here = slice(n * CAP, (n + 1) * CAP)
        saves.append(fetch(send.at[:, here], sent.at[:, here], sems.at[3 + n]))

    def first(t, carry):
        row = x_upper[pl.ds(pl.multiple_of(t * depth, depth), depth), :].astype(BF16)
        for k in range(2):
            s = slot(1, k, t)
            send[s >> 1, s & 1] = row
        return carry

    lax.fori_loop(0, tokens, first, 0, unroll=4)
    part(0)
    rows_to_tiles(grad[...].astype(F32), g_tiles, tokens, depth)

    def second(t, carry):
        g = g_tiles[pl.ds(pl.multiple_of(t * depth, depth), depth), :]
        grad_tiles[t] = g.astype(BF16)
        for k in range(2):
            s = slot(1, k, t)
            weight = jnp.where(upper, own_w[segment, k, t], other_w[segment, k, t])
            send[s >> 1, CAP + (s & 1)] = (weight * g).astype(BF16)
        return carry

    lax.fori_loop(0, tokens, second, 0, unroll=4)
    part(1)
    saves.append(fetch(grad_tiles, tiles_out, sems.at[6]))
    rows_to_tiles(jnp.where(upper, theirs, mine), x_lower, tokens, depth)

    def third(t, carry):
        row = x_lower[pl.ds(pl.multiple_of(t * depth, depth), depth), :].astype(BF16)
        for k in range(2):
            s = slot(0, k, t)
            send[s >> 1, 2 * CAP + (s & 1)] = row
        return carry

    lax.fori_loop(0, tokens, third, 0, unroll=4)
    part(2)
    for copy in saves:
        copy.wait()


def relay_kernel(
    own_slots, other_slots, own_w, other_w, back, upstream, sent, grad_out, send, sems
):
    tokens = upstream.shape[0]
    segment = lax.axis_index("segment")
    upper = segment == 1
    slot = slot_reader(own_slots, other_slots)
    clear(send, send.shape[0])

    def token(t, carry):
        total = upstream[t].astype(F32)
        for k in range(2):
            total = total + back[slot(1, k, t)].astype(F32)
        rounded = total.astype(BF16)
        grad_out[t] = rounded
        g = rounded.astype(F32)
        for k in range(2):
            weight = jnp.where(upper, other_w[segment, k, t], own_w[segment, k, t])
            send[slot(0, k, t)] = (weight * g).astype(BF16)
        return carry

    lax.fori_loop(0, tokens, token, 0, unroll=4)
    fetch(send, sent, sems.at[0]).wait()


def finish_kernel(own_slots, other_slots, back, upstream, keep, away, low, up):
    tokens, depth = upstream.shape[0], upstream.shape[1]
    upper = on_core(1)
    slot = slot_reader(own_slots, other_slots)

    def token(t, carry):
        at = pl.ds(pl.multiple_of(t * depth, depth), depth)
        g = upstream[t].astype(F32)
        up[at, :] = g
        total = g
        for k in range(2):
            total = total + back[slot(0, k, t)].astype(F32)
        low[at, :] = total
        return carry

    lax.fori_loop(0, tokens, token, 0, unroll=4)
    for j in range(depth):
        columns = slice(j * LANES, (j + 1) * LANES)
        high = up[pl.ds(j, tokens, stride=depth), :]
        down = low[pl.ds(j, tokens, stride=depth), :]
        keep[:, columns] = jnp.where(upper, high, down).astype(BF16)
        away[:, columns] = jnp.where(upper, down, high).astype(BF16)


def join_kernel(keep, came, out, sems):
    segment = lax.axis_index("segment")
    copies = [
        fetch(keep, out.at[segment], sems.at[0]),
        fetch(came, out.at[1 - segment], sems.at[1]),
    ]
    for copy in copies:
        copy.wait()


def turn_kernel(turn, gate, up, down, *refs):
    gate_up_t, down_t, a, b, c, turned, turned_down, sems = refs[-8:]
    hidden, width = down.shape
    step = 256

    def work():
        copies = [
            fetch(gate, a, sems.at[0]), fetch(up, b, sems.at[1]), fetch(down, c, sems.at[2])
        ]
        for n, block in enumerate((a, b)):
            copies[n].wait()
            for i in range(0, width, step):
                turned[n * hidden : (n + 1) * hidden, i : i + step] = block[i : i + step, :].T
        first = fetch(turned, gate_up_t, sems.at[3])
        copies[2].wait()
        for i in range(0, width, step):
            turned_down[i : i + step, :] = c[:, i : i + step].T
        fetch(turned_down, down_t, sems.at[4]).wait()
        first.wait()

    if turn is None:
        work()
    else:
        pl.when(on_core(turn))(work)


def forward_parts(tiles, gate, up, count, depth):
    number = depth // 2
    hidden_gate = hidden_up = 0.0
    for first in range(0, depth, number):
        rows = tile_columns(tiles, first, number, count, depth)
        here = slice(first * LANES, (first + number) * LANES)
        hidden_gate += jnp.dot(rows, gate[here, :], preferred_element_type=F32)
        hidden_up += jnp.dot(rows, up[here, :], preferred_element_type=F32)
    sigma = 1.0 / (1.0 + jnp.exp(-hidden_gate))
    act = hidden_gate * sigma
    dact = sigma * (1.0 + hidden_gate * (1.0 - sigma))
    return act, hidden_up * dact, (act * hidden_up).astype(BF16)


def down_part(tiles, dy_rows, down_t, depth):
    count = dy_rows.shape[0]
    number = depth // 2
    grad_act = 0.0
    for first in range(0, depth, number):
        rows = tile_columns(tiles, first, number, count, depth)
        here = slice(first * LANES, (first + number) * LANES)
        dy_rows[:, here] = rows
        grad_act += jnp.dot(rows, down_t[here, :], preferred_element_type=F32)
    return grad_act


def back_part(grad_act, act, slope, gate_up_t, tiles, send, sent, sems):
    count, depth, lanes = send.shape
    both = jnp.concatenate(
        [(grad_act * slope).astype(BF16), (grad_act * act).astype(BF16)], axis=1
    )
    number = depth // 4
    for first in range(0, depth, number):
        here = slice(first * LANES, (first + number) * LANES)
        dx = jnp.dot(both, gate_up_t[:, here], preferred_element_type=F32)
        for j in range(number):
            tiles[pl.ds(first + j, count, stride=depth), :] = dx[:, j * LANES : (j + 1) * LANES]
    pieces, copies = 4, []
    part = count // pieces
    for n in range(pieces):
        rows = tiles[n * part * depth : (n + 1) * part * depth, :]
        send[n * part : (n + 1) * part] = rows.reshape(part, depth, lanes).astype(BF16)
        here = pl.ds(n * part, part)
        copies.append(fetch(send.at[here], sent.at[here], sems.at[n]))
    return copies


def widened(block, tiles):
    tiles[...] = block[...].astype(F32).reshape(tiles.shape)


def upper_kernel(
    arrived, own_gate, other_gate, own_up, other_up, own_dt, other_dt, own_gut, other_gut,
    sent, dy_out, act_out,
    x, dy, gate, up, down_t, gate_up_t, x_tiles, dy_tiles, dx_tiles, dy_rows, activ, send, sems,
):
    mine = on_core(1)
    count, depth = send.shape[:2]
    x_copy = fetch(arrived.at[:, :CAP], x, sems.at[0])
    gate_copy = fetch_one_of(mine, own_gate, other_gate, gate, sems.at[1])
    up_copy = fetch_one_of(mine, own_up, other_up, up, sems.at[2])
    dy_copy = fetch(arrived.at[:, CAP : 2 * CAP], dy, sems.at[3])
    down_copy = fetch_one_of(mine, own_dt, other_dt, down_t, sems.at[4])
    back_copy = fetch_one_of(mine, own_gut, other_gut, gate_up_t, sems.at[5])
    x_copy.wait()
    widened(x, x_tiles)
    for copy in (gate_copy, up_copy, dy_copy, down_copy, back_copy):
        copy.wait()
    widened(dy, dy_tiles)
    act, slope, rounded = forward_parts(x_tiles, gate, up, count, depth)
    activ[...] = rounded
    grad_act = down_part(dy_tiles, dy_rows, down_t, depth)
    saves = [fetch(activ, act_out, sems.at[6]), fetch(dy_rows, dy_out, sems.at[7])]
    saves += back_part(
        grad_act, act, slope, gate_up_t, dx_tiles, send, sent, sems.at[pl.ds(8, 4)]
    )
    for copy in saves:
        copy.wait()


def forward_kernel(
    arrived, own_gate, other_gate, own_up, other_up, act_out, slope_out, activ_out,
    x, gate, up, tiles, sems,
):
    mine = on_core(0)
    experts, cap, depth = x.shape[:3]
    x_copy = fetch(arrived.at[:, 2 * CAP :], x, sems.at[0])
    gate_copy = fetch_one_of(mine, own_gate, other_gate, gate, sems.at[1])
    up_copy = fetch_one_of(mine, own_up, other_up, up, sems.at[2])
    x_copy.wait()
    widened(x, tiles)
    gate_copy.wait()
    up_copy.wait()
    act, slope, rounded = forward_parts(tiles, gate, up, experts * cap, depth)
    act_out[...] = act
    slope_out[...] = slope
    activ_out[...] = rounded


def lower_kernel(
    dy_in, act_in, slope_in, own_dt, other_dt, own_gut, other_gut, sent, dy_out,
    dy, act, slope, down_t, gate_up_t, dy_tiles, dx_tiles, dy_rows, send, sems,
):
    mine = on_core(0)
    count, depth = send.shape[:2]
    pieces = 4
    part = count // pieces
    arriving = [
        fetch(dy_in.at[pl.ds(n * part, part)], dy.at[pl.ds(n * part, part)], sems.at[9 + n])
        for n in range(pieces)
    ]
    down_copy = fetch_one_of(mine, own_dt, other_dt, down_t, sems.at[0])
    act_copy = fetch(act_in, act, sems.at[1])
    slope_copy = fetch(slope_in, slope, sems.at[2])
    back_copy = fetch_one_of(mine, own_gut, other_gut, gate_up_t, sems.at[3])
    for n, copy in enumerate(arriving):
        copy.wait()
        dy_tiles[n * part * depth : (n + 1) * part * depth, :] = (
            dy[n * part : (n + 1) * part].astype(F32).reshape(part * depth, LANES)
        )
    for copy in (down_copy, act_copy, slope_copy, back_copy):
        copy.wait()
    grad_act = down_part(dy_tiles, dy_rows, down_t, depth)
    saves = [fetch(dy_rows, dy_out, sems.at[4])]
    saves += back_part(
        grad_act, act[...], slope[...], gate_up_t, dx_tiles, send, sent, sems.at[pl.ds(5, 4)]
    )
    for copy in saves:
        copy.wait()


def call(kernel, args, in_specs, out_shape, out_specs, scratch, flops, moved, aliases={}):
    return pl.pallas_call(
        kernel,
        in_specs=in_specs,
        out_shape=out_shape,
        out_specs=out_specs,
        scratch_shapes=scratch,
        input_output_aliases=aliases,
        compiler_params=pltpu.CompilerParams(vmem_limit_bytes=63 * 1024 * 1024),
        cost_estimate=pl.CostEstimate(flops=flops, bytes_accessed=moved, transcendentals=0),
    )(*args)


def swapped(block):
    return lax.ppermute(block, "segment", [(0, 1), (1, 0)])


def exchanged(block):
    return lax.all_to_all(block, "expert", split_axis=0, concat_axis=0, tiled=True)


def shape(dims, kind=BF16):
    return jax.ShapeDtypeStruct(dims, kind)


def shards(saved_input, out_grad, expert_ids, router_weights, w_gate, w_up, w_down, eigenbasis):
    experts = lax.axis_size("expert")
    segment = lax.axis_index("segment")
    upper = segment == 1
    micros, tokens, width = saved_input.shape[1:]
    hidden = w_gate.shape[-1]
    depth = width // LANES
    count = experts * CAP
    gate, up, down, basis = w_gate[0, 0], w_up[0, 0], w_down[0, 0], eigenbasis[0, 0]

    other_x = swapped(
        lax.dynamic_index_in_dim(saved_input[0], 1 - segment, 0, keepdims=False)
    )
    ids = jnp.swapaxes(expert_ids[0], 1, 2)
    own_w = jnp.swapaxes(router_weights[0], 1, 2)
    order = 2 * np.arange(tokens)[None, :] + np.arange(2)[:, None]
    earlier = order[None, None] < order[..., None, None]
    same = ids[:, None, None] == ids[..., None, None]
    rank = jnp.sum((same & earlier[None]).astype(jnp.int32), axis=(3, 4))
    own_slots = ids * CAP + jnp.minimum(rank, CAP - 1)
    other_slots, other_w = swapped(own_slots), swapped(own_w)

    matrix = pltpu.VMEM((width, hidden), BF16)
    turned_shapes = (shape((2 * hidden, width)), shape((width, hidden)))
    turn_scratch = [
        matrix, matrix, pltpu.VMEM((hidden, width), BF16), pltpu.VMEM((2 * hidden, width), BF16),
        matrix, pltpu.SemaphoreType.DMA((5,)),
    ]

    def turned(turn, matrices, made=()):
        return call(
            functools.partial(turn_kernel, turn),
            (*matrices, *made),
            [HBM] * (3 + len(made)),
            turned_shapes,
            (HBM,) * 2,
            turn_scratch,
            1_000_000,
            9_000_000,
            {3: 0, 4: 1} if made else {},
        )

    early_gut, early_dt = turned(0, (gate, up, down))

    tile_rows = tokens * depth
    row_block = pltpu.VMEM((tokens, width), BF16)
    send, grad_tiles = call(
        dispatch_kernel,
        (own_slots, other_slots, own_w, other_w, saved_input[0], other_x, out_grad, early_dt),
        [SMEM] * 4 + [HBM] * 4,
        (shape((experts, 3 * CAP, depth, LANES)), shape((tokens, depth, LANES))),
        (HBM,) * 2,
        [
            pltpu.VMEM((experts, 3 * CAP, depth, LANES), BF16),
            pltpu.VMEM((tokens, depth, LANES), BF16),
        ]
        + [row_block] * 3
        + [pltpu.VMEM((tile_rows, LANES), F32)] * 3
        + [pltpu.SemaphoreType.DMA((7,))],
        1_000_000,
        5_000_000,
    )
    arrived = exchanged(send)

    own_gut, own_dt = turned(1, (gate, up, down), (early_gut, early_dt))
    other_gate, other_up, other_down = swapped(gate), swapped(up), swapped(down)
    other_basis = swapped(basis)
    other_gut, other_dt = turned(None, (other_gate, other_up, other_down))

    tiles = pltpu.VMEM((count * depth, LANES), F32)
    rows = pltpu.VMEM((count, width), BF16)
    part = pltpu.VMEM((experts, CAP, depth, LANES), BF16)
    flat = (count, depth, LANES)
    flat_scratch = pltpu.VMEM(flat, BF16)
    mat = 2 * count * width * hidden
    back_send, dy_rows1, activ1 = call(
        upper_kernel,
        (arrived, gate, other_gate, up, other_up, own_dt, other_dt, own_gut, other_gut),
        [HBM] * 9,
        (shape(flat), shape((count, width)), shape((count, hidden))),
        (HBM,) * 3,
        [
            part, part, matrix, matrix, matrix, pltpu.VMEM((2 * hidden, width), BF16), tiles,
            tiles, tiles, rows, pltpu.VMEM((count, hidden), BF16), flat_scratch,
            pltpu.SemaphoreType.DMA((12,)),
        ],
        5 * mat,
        9_000_000,
    )

    def returned(block):
        return exchanged(block.reshape(experts, CAP, depth, LANES)).reshape(flat)

    back = returned(back_send)
    act0, slope0, activ0 = call(
        forward_kernel,
        (arrived, gate, other_gate, up, other_up),
        [HBM] * 5,
        (shape((count, hidden), F32), shape((count, hidden), F32), shape((count, hidden))),
        (VMEM,) * 3,
        [part, matrix, matrix, tiles, pltpu.SemaphoreType.DMA((3,))],
        2 * mat,
        5_000_000,
    )
    basis1 = jnp.where(upper, basis, other_basis)
    basis0 = jnp.where(upper, other_basis, basis)
    rotated1 = jnp.dot(activ1, basis1, preferred_element_type=F32).astype(BF16)
    rotated0 = jnp.dot(activ0, basis0, preferred_element_type=F32).astype(BF16)

    dy_send, grad1 = call(
        relay_kernel,
        (own_slots, other_slots, own_w, other_w, back, grad_tiles),
        [SMEM] * 4 + [VMEM] * 2,
        (shape(flat), shape((tokens, depth, LANES))),
        (HBM, VMEM),
        [flat_scratch, pltpu.SemaphoreType.DMA((1,))],
        1_000_000,
        3_000_000,
    )
    dy = returned(dy_send)
    back_send0, dy_rows0 = call(
        lower_kernel,
        (dy, act0, slope0, own_dt, other_dt, own_gut, other_gut),
        [HBM] * 7,
        (shape(flat), shape((count, width))),
        (HBM,) * 2,
        [
            flat_scratch, pltpu.VMEM((count, hidden), F32), pltpu.VMEM((count, hidden), F32),
            matrix, pltpu.VMEM((2 * hidden, width), BF16), tiles, tiles, rows, flat_scratch,
            pltpu.SemaphoreType.DMA((13,)),
        ],
        3 * mat,
        8_000_000,
    )
    back0 = returned(back_send0)

    all_rotated = jnp.concatenate(
        [
            jnp.where(upper, rotated1, rotated0),
            swapped(jnp.where(upper, rotated0, rotated1)),
        ],
        axis=0,
    )
    all_dy = jnp.concatenate(
        [
            jnp.where(upper, dy_rows1, dy_rows0),
            swapped(jnp.where(upper, dy_rows0, dy_rows1)),
        ],
        axis=0,
    )
    rot_sq = (all_rotated.astype(F32) ** 2).astype(BF16)
    dy_sq = (all_dy.astype(F32) ** 2).astype(BF16)
    over_rows = (((0,), (0,)), ((), ()))
    grad_sum = lax.dot_general(all_rotated, all_dy, over_rows, preferred_element_type=F32)
    scale_sum = lax.dot_general(rot_sq, dy_sq, over_rows, preferred_element_type=F32)
    rotated_grad = (grad_sum * (1.0 / micros)).astype(BF16)
    ekfac_scales = scale_sum * (1.0 / micros)
    back0, rotated_grad, ekfac_scales = lax.optimization_barrier(
        (back0, rotated_grad, ekfac_scales)
    )

    keep, away = call(
        finish_kernel,
        (own_slots, other_slots, back0, grad1),
        [SMEM] * 2 + [VMEM] * 2,
        (shape((tokens, width)), shape((tokens, width))),
        (VMEM,) * 2,
        [pltpu.VMEM((tile_rows, LANES), F32)] * 2,
        1_000_000,
        2_000_000,
    )
    came = swapped(away)
    grads = call(
        join_kernel,
        (keep, came),
        [HBM] * 2,
        shape((micros, tokens, width)),
        HBM,
        [pltpu.SemaphoreType.DMA((2,))],
        0,
        1_000_000,
    )
    return (grads[None], rotated_grad[None, None], ekfac_scales[None, None])


def solution(mesh):
    in_specs = (
        P("segment", None, "expert", None),
        P(None, "expert", None),
        P("segment", None, "expert", None),
        P("segment", None, "expert", None),
        P("segment", "expert", None, None),
        P("segment", "expert", None, None),
        P("segment", "expert", None, None),
        P("segment", "expert", None, None),
    )
    out_specs = (
        P("segment", None, "expert", None),
        P("segment", "expert", None, None),
        P("segment", "expert", None, None),
    )
    return jax.shard_map(shards, mesh=mesh, in_specs=in_specs, out_specs=out_specs, check_vma=False)
```

```python
import functools
import jax
import jax.numpy as jnp
import numpy as np
from jax import lax
from jax.experimental import pallas as pl
from jax.experimental.pallas import tpu as pltpu
from jax.sharding import PartitionSpec as P

LANES = 128
CAP = 2
F32 = jnp.float32
BF16 = jnp.bfloat16
SMEM = pl.BlockSpec(memory_space=pltpu.SMEM)
VMEM = pl.BlockSpec(memory_space=pltpu.VMEM)
HBM = pl.BlockSpec(memory_space=pltpu.HBM)
VMEM_MIB = 28


def rows_to_tiles(rows, tiles, count, depth):
    for j in range(depth):
        tiles[pl.ds(j, count, stride=depth), :] = rows[:, j * LANES : (j + 1) * LANES]


def tiles_to_rows(tiles, rows, count, depth):
    for j in range(depth):
        rows[:, j * LANES : (j + 1) * LANES] = tiles[pl.ds(j, count, stride=depth), :].astype(
            rows.dtype
        )


def clear(send, experts):
    zero = jnp.zeros(send.shape[1:], send.dtype)

    def one(e, carry):
        send[e] = zero
        return carry

    lax.fori_loop(0, experts, one, 0, unroll=8)


def on_core(which):
    return lax.axis_index("segment") == which


def fetch(source, target, sem):
    copy = pltpu.make_async_copy(source, target, sem)
    copy.start()
    return copy


def fetch_one_of(first, own, other, target, sem):
    @pl.when(first)
    def _():
        pltpu.make_async_copy(own, target, sem).start()

    @pl.when(jnp.logical_not(first))
    def _():
        pltpu.make_async_copy(other, target, sem).start()

    return pltpu.make_async_copy(own, target, sem)


def slot_reader(own_slots, other_slots):
    segment = lax.axis_index("segment")

    def slot(layer, k, t):
        mine, theirs = own_slots[segment, k, t], other_slots[segment, k, t]
        return jnp.where(segment == layer, mine, theirs)

    return slot


def dispatch_kernel(
    own_slots, other_slots, own_w, other_w, own_x, other_x, grads, after, sent, tiles_out,
    send, grad_tiles, own, other, grad, x_upper, x_lower, g_tiles, sems,
):
    tokens, width = grad.shape
    depth = width // LANES
    segment = lax.axis_index("segment")
    upper = segment == 1
    slot = slot_reader(own_slots, other_slots)
    copies = [
        fetch(own_x.at[segment], own, sems.at[0]),
        fetch(other_x, other, sems.at[1]),
        fetch(grads.at[segment], grad, sems.at[2]),
    ]
    clear(send, send.shape[0])
    for copy in copies:
        copy.wait()
    mine, theirs = own[...].astype(F32), other[...].astype(F32)
    rows_to_tiles(jnp.where(upper, mine, theirs), x_upper, tokens, depth)
    saves = []

    def part(n):
        here = slice(n * CAP, (n + 1) * CAP)
        saves.append(fetch(send.at[:, here], sent.at[:, here], sems.at[3 + n]))

    def first(t, carry):
        row = x_upper[pl.ds(pl.multiple_of(t * depth, depth), depth), :].astype(BF16)
        for k in range(2):
            s = slot(1, k, t)
            send[s >> 1, s & 1] = row
        return carry

    lax.fori_loop(0, tokens, first, 0, unroll=4)
    part(0)
    rows_to_tiles(grad[...].astype(F32), g_tiles, tokens, depth)

    def second(t, carry):
        g = g_tiles[pl.ds(pl.multiple_of(t * depth, depth), depth), :]
        grad_tiles[t] = g.astype(BF16)
        for k in range(2):
            s = slot(1, k, t)
            weight = jnp.where(upper, own_w[segment, k, t], other_w[segment, k, t])
            send[s >> 1, CAP + (s & 1)] = (weight * g).astype(BF16)
        return carry

    lax.fori_loop(0, tokens, second, 0, unroll=4)
    part(1)
    saves.append(fetch(grad_tiles, tiles_out, sems.at[6]))
    rows_to_tiles(jnp.where(upper, theirs, mine), x_lower, tokens, depth)

    def third(t, carry):
        row = x_lower[pl.ds(pl.multiple_of(t * depth, depth), depth), :].astype(BF16)
        for k in range(2):
            s = slot(0, k, t)
            send[s >> 1, 2 * CAP + (s & 1)] = row
        return carry

    lax.fori_loop(0, tokens, third, 0, unroll=4)
    part(2)
    for copy in saves:
        copy.wait()


def relay_kernel(
    own_slots, other_slots, own_w, other_w, back, upstream, sent, grad_out, send, sems
):
    tokens = upstream.shape[0]
    segment = lax.axis_index("segment")
    upper = segment == 1
    slot = slot_reader(own_slots, other_slots)
    clear(send, send.shape[0])

    def token(t, carry):
        total = upstream[t].astype(F32)
        for k in range(2):
            total = total + back[slot(1, k, t)].astype(F32)
        rounded = total.astype(BF16)
        grad_out[t] = rounded
        g = rounded.astype(F32)
        for k in range(2):
            weight = jnp.where(upper, other_w[segment, k, t], own_w[segment, k, t])
            send[slot(0, k, t)] = (weight * g).astype(BF16)
        return carry

    lax.fori_loop(0, tokens, token, 0, unroll=4)
    fetch(send, sent, sems.at[0]).wait()


def finish_kernel(own_slots, other_slots, back, upstream, out, away, keep, low, up, sems):
    tokens, depth = upstream.shape[0], upstream.shape[1]
    upper = on_core(1)
    slot = slot_reader(own_slots, other_slots)

    def token(t, carry):
        at = pl.ds(pl.multiple_of(t * depth, depth), depth)
        g = upstream[t].astype(F32)
        up[at, :] = g
        total = g
        for k in range(2):
            total = total + back[slot(0, k, t)].astype(F32)
        low[at, :] = total
        return carry

    lax.fori_loop(0, tokens, token, 0, unroll=4)
    for j in range(depth):
        columns = slice(j * LANES, (j + 1) * LANES)
        high = up[pl.ds(j, tokens, stride=depth), :]
        down = low[pl.ds(j, tokens, stride=depth), :]
        keep[:, columns] = jnp.where(upper, high, down).astype(BF16)
        away[:, columns] = jnp.where(upper, down, high).astype(BF16)
    fetch(keep, out.at[lax.axis_index("segment")], sems.at[0]).wait()


def join_kernel(came, partial, out, sems):
    fetch(came, out.at[1 - lax.axis_index("segment")], sems.at[0]).wait()


def turn_kernel(turn, gate, up, down, *refs):
    gate_up_t, down_t, a, b, c, turned, turned_down, sems = refs[-8:]
    hidden, width = down.shape
    step = 256

    def work():
        copies = [
            fetch(gate, a, sems.at[0]), fetch(up, b, sems.at[1]), fetch(down, c, sems.at[2])
        ]
        for n, block in enumerate((a, b)):
            copies[n].wait()
            for i in range(0, width, step):
                turned[n * hidden : (n + 1) * hidden, i : i + step] = block[i : i + step, :].T
        first = fetch(turned, gate_up_t, sems.at[3])
        copies[2].wait()
        for i in range(0, width, step):
            turned_down[i : i + step, :] = c[:, i : i + step].T
        fetch(turned_down, down_t, sems.at[4]).wait()
        first.wait()

    if turn is None:
        work()
    else:
        pl.when(on_core(turn))(work)


def forward_parts(rows, gate, up):
    hidden_gate = jnp.dot(rows[...], gate[...], preferred_element_type=F32)
    hidden_up = jnp.dot(rows[...], up[...], preferred_element_type=F32)
    sigma = 1.0 / (1.0 + jnp.exp(-hidden_gate))
    act = hidden_gate * sigma
    dact = sigma * (1.0 + hidden_gate * (1.0 - sigma))
    return act, hidden_up * dact, (act * hidden_up).astype(BF16)


def back_part(grad_act, act, slope, gate_up_t, tiles, send, sent, sems):
    count, depth, lanes = send.shape
    both = jnp.concatenate(
        [(grad_act * slope).astype(BF16), (grad_act * act).astype(BF16)], axis=1
    )
    dx = jnp.dot(both, gate_up_t[...], preferred_element_type=F32)
    rows_to_tiles(dx, tiles, count, depth)
    pieces, copies = 4, []
    part = count // pieces
    for n in range(pieces):
        rows = tiles[n * part * depth : (n + 1) * part * depth, :]
        send[n * part : (n + 1) * part] = rows.reshape(part, depth, lanes).astype(BF16)
        here = pl.ds(n * part, part)
        copies.append(fetch(send.at[here], sent.at[here], sems.at[n]))
    return copies


def untile(block, tiles, rows, depth):
    count = rows.shape[0]
    tiles[...] = block.astype(F32).reshape(count * depth, LANES)
    tiles_to_rows(tiles, rows, count, depth)


def upper_kernel(
    arrived, own_gate, other_gate, own_up, other_up, own_dt, other_dt, own_gut, other_gut,
    sent, dy_out, act_out,
    gate, up, down_t, gate_up_t, tiles, x_rows, dy_rows, activ, send, sems,
):
    mine = on_core(1)
    depth = send.shape[1]
    gate_copy = fetch_one_of(mine, own_gate, other_gate, gate, sems.at[0])
    up_copy = fetch_one_of(mine, own_up, other_up, up, sems.at[1])
    down_copy = fetch_one_of(mine, own_dt, other_dt, down_t, sems.at[2])
    back_copy = fetch_one_of(mine, own_gut, other_gut, gate_up_t, sems.at[3])
    untile(arrived[:, :CAP], tiles, x_rows, depth)
    gate_copy.wait()
    up_copy.wait()
    act, slope, rounded = forward_parts(x_rows, gate, up)
    activ[...] = rounded
    untile(arrived[:, CAP : 2 * CAP], tiles, dy_rows, depth)
    saves = [fetch(activ, act_out, sems.at[4]), fetch(dy_rows, dy_out, sems.at[5])]
    down_copy.wait()
    grad_act = jnp.dot(dy_rows[...], down_t[...], preferred_element_type=F32)
    back_copy.wait()
    saves += back_part(grad_act, act, slope, gate_up_t, tiles, send, sent, sems.at[pl.ds(6, 4)])
    for copy in saves:
        copy.wait()


def forward_kernel(
    arrived, own_gate, other_gate, own_up, other_up, act_out, slope_out, activ_out,
    act, slope, activ, gate, up, tiles, x_rows, sems,
):
    mine = on_core(0)
    depth = arrived.shape[2]
    gate_copy = fetch_one_of(mine, own_gate, other_gate, gate, sems.at[0])
    up_copy = fetch_one_of(mine, own_up, other_up, up, sems.at[1])
    untile(arrived[:, 2 * CAP :], tiles, x_rows, depth)
    gate_copy.wait()
    up_copy.wait()
    act[...], slope[...], activ[...] = forward_parts(x_rows, gate, up)
    saves = [
        fetch(act, act_out, sems.at[2]),
        fetch(slope, slope_out, sems.at[3]),
        fetch(activ, activ_out, sems.at[4]),
    ]
    for copy in saves:
        copy.wait()


def lower_kernel(
    dy, act_in, slope_in, own_dt, other_dt, own_gut, other_gut, sent, dy_out,
    act, slope, down_t, gate_up_t, tiles, dy_rows, send, sems,
):
    mine = on_core(0)
    down_copy = fetch_one_of(mine, own_dt, other_dt, down_t, sems.at[0])
    act_copy = fetch(act_in, act, sems.at[1])
    slope_copy = fetch(slope_in, slope, sems.at[2])
    back_copy = fetch_one_of(mine, own_gut, other_gut, gate_up_t, sems.at[3])
    untile(dy[...], tiles, dy_rows, send.shape[1])
    saves = [fetch(dy_rows, dy_out, sems.at[4])]
    down_copy.wait()
    grad_act = jnp.dot(dy_rows[...], down_t[...], preferred_element_type=F32)
    for copy in (act_copy, slope_copy, back_copy):
        copy.wait()
    saves += back_part(
        grad_act, act[...], slope[...], gate_up_t, tiles, send, sent, sems.at[pl.ds(5, 4)]
    )
    for copy in saves:
        copy.wait()


INPLACE = pl.BlockSpec(memory_space=pltpu.VMEM)


def placed(arg, spec):
    if spec is HBM:
        return pltpu.with_memory_space_constraint(arg, pltpu.HBM)
    if spec is INPLACE:
        return pltpu.with_memory_space_constraint(arg, pltpu.VMEM)
    return arg


def call(kernel, args, in_specs, out_shape, out_specs, scratch, flops, moved, aliases={}):
    return pl.pallas_call(
        kernel,
        in_specs=in_specs,
        out_shape=tuple(
            pltpu.HBM(out.shape, out.dtype) if spec is HBM else out
            for out, spec in zip(out_shape, out_specs)
        ),
        out_specs=out_specs,
        scratch_shapes=scratch,
        input_output_aliases=aliases,
        compiler_params=pltpu.CompilerParams(vmem_limit_bytes=VMEM_MIB * 1024 * 1024),
        cost_estimate=pl.CostEstimate(flops=flops, bytes_accessed=moved, transcendentals=0),
    )(*[placed(arg, spec) for arg, spec in zip(args, in_specs)])


def swapped(block):
    return lax.ppermute(block, "segment", [(0, 1), (1, 0)])


def exchanged(block):
    return lax.all_to_all(block, "expert", split_axis=0, concat_axis=0, tiled=True)


def shape(dims, kind=BF16):
    return jax.ShapeDtypeStruct(dims, kind)


def shards(saved_input, out_grad, expert_ids, router_weights, w_gate, w_up, w_down, eigenbasis):
    experts = lax.axis_size("expert")
    segment = lax.axis_index("segment")
    upper = segment == 1
    micros, tokens, width = saved_input.shape[1:]
    hidden = w_gate.shape[-1]
    depth = width // LANES
    count = experts * CAP
    gate, up, down, basis = w_gate[0, 0], w_up[0, 0], w_down[0, 0], eigenbasis[0, 0]

    other_x = swapped(
        lax.dynamic_index_in_dim(saved_input[0], 1 - segment, 0, keepdims=False)
    )
    ids = jnp.swapaxes(expert_ids[0], 1, 2)
    own_w = jnp.swapaxes(router_weights[0], 1, 2)
    order = 2 * np.arange(tokens)[None, :] + np.arange(2)[:, None]
    earlier = order[None, None] < order[..., None, None]
    same = ids[:, None, None] == ids[..., None, None]
    rank = jnp.sum((same & earlier[None]).astype(jnp.int32), axis=(3, 4))
    own_slots = ids * CAP + jnp.minimum(rank, CAP - 1)
    other_slots, other_w = swapped(own_slots), swapped(own_w)

    matrix = pltpu.VMEM((width, hidden), BF16)
    turned_shapes = (shape((2 * hidden, width)), shape((width, hidden)))
    turn_scratch = [
        matrix, matrix, pltpu.VMEM((hidden, width), BF16), pltpu.VMEM((2 * hidden, width), BF16),
        matrix, pltpu.SemaphoreType.DMA((5,)),
    ]

    def turned(turn, matrices, made=()):
        return call(
            functools.partial(turn_kernel, turn),
            (*matrices, *made),
            [HBM] * (3 + len(made)),
            turned_shapes,
            (HBM,) * 2,
            turn_scratch,
            1_000_000,
            9_000_000,
            {3: 0, 4: 1} if made else {},
        )

    early_gut, early_dt = turned(0, (gate, up, down))

    tile_rows = tokens * depth
    row_block = pltpu.VMEM((tokens, width), BF16)
    send, grad_tiles = call(
        dispatch_kernel,
        (own_slots, other_slots, own_w, other_w, saved_input[0], other_x, out_grad, early_dt),
        [SMEM] * 4 + [HBM] * 4,
        (shape((experts, 3 * CAP, depth, LANES)), shape((tokens, depth, LANES))),
        (HBM,) * 2,
        [
            pltpu.VMEM((experts, 3 * CAP, depth, LANES), BF16),
            pltpu.VMEM((tokens, depth, LANES), BF16),
        ]
        + [row_block] * 3
        + [pltpu.VMEM((tile_rows, LANES), F32)] * 3
        + [pltpu.SemaphoreType.DMA((7,))],
        1_000_000,
        5_000_000,
    )
    arrived = exchanged(send)

    own_gut, own_dt = turned(1, (gate, up, down), (early_gut, early_dt))
    other_gate, other_up, other_down = swapped(gate), swapped(up), swapped(down)
    other_basis = swapped(basis)
    other_gut, other_dt = turned(None, (other_gate, other_up, other_down))

    tiles = pltpu.VMEM((count * depth, LANES), F32)
    rows = pltpu.VMEM((count, width), BF16)
    flat = (count, depth, LANES)
    flat_scratch = pltpu.VMEM(flat, BF16)
    mat = 2 * count * width * hidden
    back_send, dy_rows1, activ1 = call(
        upper_kernel,
        (arrived, gate, other_gate, up, other_up, own_dt, other_dt, own_gut, other_gut),
        [INPLACE] + [HBM] * 8,
        (shape(flat), shape((count, width)), shape((count, hidden))),
        (HBM,) * 3,
        [
            matrix, matrix, matrix, pltpu.VMEM((2 * hidden, width), BF16), tiles,
            rows, rows, pltpu.VMEM((count, hidden), BF16), flat_scratch,
            pltpu.SemaphoreType.DMA((10,)),
        ],
        5 * mat,
        9_000_000,
    )

    def returned(block):
        return exchanged(block.reshape(experts, CAP, depth, LANES)).reshape(flat)

    back = returned(back_send)
    act0, slope0, activ0 = call(
        forward_kernel,
        (arrived, gate, other_gate, up, other_up),
        [INPLACE] + [HBM] * 4,
        (shape((count, hidden), F32), shape((count, hidden), F32), shape((count, hidden))),
        (HBM,) * 3,
        [
            pltpu.VMEM((count, hidden), F32), pltpu.VMEM((count, hidden), F32),
            pltpu.VMEM((count, hidden), BF16), matrix, matrix, tiles, rows,
            pltpu.SemaphoreType.DMA((5,)),
        ],
        2 * mat,
        5_000_000,
    )
    basis1 = jnp.where(upper, basis, other_basis)
    basis0 = jnp.where(upper, other_basis, basis)
    rotated1 = jnp.dot(activ1, basis1, preferred_element_type=F32).astype(BF16)
    rotated0 = jnp.dot(activ0, basis0, preferred_element_type=F32).astype(BF16)

    dy_send, grad1 = call(
        relay_kernel,
        (own_slots, other_slots, own_w, other_w, back, grad_tiles),
        [SMEM] * 4 + [INPLACE, VMEM],
        (shape(flat), shape((tokens, depth, LANES))),
        (HBM, VMEM),
        [flat_scratch, pltpu.SemaphoreType.DMA((1,))],
        1_000_000,
        3_000_000,
    )
    dy = returned(dy_send)
    back_send0, dy_rows0 = call(
        lower_kernel,
        (dy, act0, slope0, own_dt, other_dt, own_gut, other_gut),
        [INPLACE] + [HBM] * 6,
        (shape(flat), shape((count, width))),
        (HBM,) * 2,
        [
            pltpu.VMEM((count, hidden), F32), pltpu.VMEM((count, hidden), F32),
            matrix, pltpu.VMEM((2 * hidden, width), BF16), tiles, rows, flat_scratch,
            pltpu.SemaphoreType.DMA((9,)),
        ],
        3 * mat,
        8_000_000,
    )
    back0 = returned(back_send0)

    all_rotated = jnp.concatenate(
        [
            jnp.where(upper, rotated1, rotated0),
            swapped(jnp.where(upper, rotated0, rotated1)),
        ],
        axis=0,
    )
    all_dy = jnp.concatenate(
        [
            jnp.where(upper, dy_rows1, dy_rows0),
            swapped(jnp.where(upper, dy_rows0, dy_rows1)),
        ],
        axis=0,
    )
    rot_sq = (all_rotated.astype(F32) ** 2).astype(BF16)
    dy_sq = (all_dy.astype(F32) ** 2).astype(BF16)
    over_rows = (((0,), (0,)), ((), ()))
    grad_sum = lax.dot_general(all_rotated, all_dy, over_rows, preferred_element_type=F32)
    scale_sum = lax.dot_general(rot_sq, dy_sq, over_rows, preferred_element_type=F32)
    rotated_grad = (grad_sum * (1.0 / micros)).astype(BF16)
    ekfac_scales = scale_sum * (1.0 / micros)
    back0, rotated_grad, ekfac_scales = lax.optimization_barrier(
        (back0, rotated_grad, ekfac_scales)
    )

    own_grads, away = call(
        finish_kernel,
        (own_slots, other_slots, back0, grad1),
        [SMEM] * 2 + [INPLACE, VMEM],
        (shape((micros, tokens, width)), shape((tokens, width))),
        (HBM, VMEM),
        [row_block]
        + [pltpu.VMEM((tile_rows, LANES), F32)] * 2
        + [pltpu.SemaphoreType.DMA((1,))],
        1_000_000,
        2_000_000,
    )
    (grads,) = call(
        join_kernel,
        (swapped(away), own_grads),
        [INPLACE, HBM],
        (shape((micros, tokens, width)),),
        (HBM,),
        [pltpu.SemaphoreType.DMA((1,))],
        0,
        1_000_000,
        {1: 0},
    )
    return (grads[None], rotated_grad[None, None], ekfac_scales[None, None])


def solution(mesh):
    in_specs = (
        P("segment", None, "expert", None),
        P(None, "expert", None),
        P("segment", None, "expert", None),
        P("segment", None, "expert", None),
        P("segment", "expert", None, None),
        P("segment", "expert", None, None),
        P("segment", "expert", None, None),
        P("segment", "expert", None, None),
    )
    out_specs = (
        P("segment", None, "expert", None),
        P("segment", "expert", None, None),
        P("segment", "expert", None, None),
    )
    return jax.shard_map(shards, mesh=mesh, in_specs=in_specs, out_specs=out_specs, check_vma=False)
```

```python
import functools
import jax
import jax.numpy as jnp
import numpy as np
from jax import lax
from jax.experimental import pallas as pl
from jax.experimental.pallas import tpu as pltpu
from jax.sharding import PartitionSpec as P

LANES = 128
CAP = 2
F32 = jnp.float32
BF16 = jnp.bfloat16
SMEM = pl.BlockSpec(memory_space=pltpu.SMEM)
VMEM = pl.BlockSpec(memory_space=pltpu.VMEM)
HBM = pl.BlockSpec(memory_space=pltpu.HBM)
VMEM_MIB = 28


def rows_to_tiles(rows, tiles, count, depth):
    for j in range(depth):
        tiles[pl.ds(j, count, stride=depth), :] = rows[:, j * LANES : (j + 1) * LANES]


def tiles_to_rows(tiles, rows, count, depth):
    for j in range(depth):
        rows[:, j * LANES : (j + 1) * LANES] = tiles[pl.ds(j, count, stride=depth), :].astype(
            rows.dtype
        )


def clear(send, experts):
    zero = jnp.zeros(send.shape[1:], send.dtype)

    def one(e, carry):
        send[e] = zero
        return carry

    lax.fori_loop(0, experts, one, 0, unroll=8)


def on_core(which):
    return lax.axis_index("segment") == which


def fetch(source, target, sem):
    copy = pltpu.make_async_copy(source, target, sem)
    copy.start()
    return copy


def fetch_one_of(first, own, other, target, sem):
    @pl.when(first)
    def _():
        pltpu.make_async_copy(own, target, sem).start()

    @pl.when(jnp.logical_not(first))
    def _():
        pltpu.make_async_copy(other, target, sem).start()

    return pltpu.make_async_copy(own, target, sem)


def slot_reader(own_slots, other_slots):
    segment = lax.axis_index("segment")

    def slot(layer, k, t):
        mine, theirs = own_slots[segment, k, t], other_slots[segment, k, t]
        return jnp.where(segment == layer, mine, theirs)

    return slot


def dispatch_kernel(
    own_slots, other_slots, own_w, other_w, own_x, other_x, grads, after, sent, tiles_out,
    send, grad_tiles, own, other, grad, x_upper, x_lower, g_tiles, sems,
):
    tokens, width = grad.shape
    depth = width // LANES
    segment = lax.axis_index("segment")
    upper = segment == 1
    slot = slot_reader(own_slots, other_slots)
    copies = [
        fetch(own_x.at[segment], own, sems.at[0]),
        fetch(other_x, other, sems.at[1]),
        fetch(grads.at[segment], grad, sems.at[2]),
    ]
    clear(send, send.shape[0])
    for copy in copies:
        copy.wait()
    mine, theirs = own[...].astype(F32), other[...].astype(F32)
    rows_to_tiles(jnp.where(upper, mine, theirs), x_upper, tokens, depth)
    saves = []

    def part(n):
        here = slice(n * CAP, (n + 1) * CAP)
        saves.append(fetch(send.at[:, here], sent.at[:, here], sems.at[3 + n]))

    def first(t, carry):
        row = x_upper[pl.ds(pl.multiple_of(t * depth, depth), depth), :].astype(BF16)
        for k in range(2):
            s = slot(1, k, t)
            send[s >> 1, s & 1] = row
        return carry

    lax.fori_loop(0, tokens, first, 0, unroll=4)
    part(0)
    rows_to_tiles(grad[...].astype(F32), g_tiles, tokens, depth)

    def second(t, carry):
        g = g_tiles[pl.ds(pl.multiple_of(t * depth, depth), depth), :]
        grad_tiles[t] = g.astype(BF16)
        for k in range(2):
            s = slot(1, k, t)
            weight = jnp.where(upper, own_w[segment, k, t], other_w[segment, k, t])
            send[s >> 1, CAP + (s & 1)] = (weight * g).astype(BF16)
        return carry

    lax.fori_loop(0, tokens, second, 0, unroll=4)
    part(1)
    saves.append(fetch(grad_tiles, tiles_out, sems.at[6]))
    rows_to_tiles(jnp.where(upper, theirs, mine), x_lower, tokens, depth)

    def third(t, carry):
        row = x_lower[pl.ds(pl.multiple_of(t * depth, depth), depth), :].astype(BF16)
        for k in range(2):
            s = slot(0, k, t)
            send[s >> 1, 2 * CAP + (s & 1)] = row
        return carry

    lax.fori_loop(0, tokens, third, 0, unroll=4)
    part(2)
    for copy in saves:
        copy.wait()


def relay_kernel(
    own_slots, other_slots, own_w, other_w, back, upstream, sent, grad_out, send, sems
):
    tokens = upstream.shape[0]
    segment = lax.axis_index("segment")
    upper = segment == 1
    slot = slot_reader(own_slots, other_slots)
    clear(send, send.shape[0])

    def token(t, carry):
        total = upstream[t].astype(F32)
        for k in range(2):
            total = total + back[slot(1, k, t)].astype(F32)
        rounded = total.astype(BF16)
        grad_out[t] = rounded
        g = rounded.astype(F32)
        for k in range(2):
            weight = jnp.where(upper, other_w[segment, k, t], own_w[segment, k, t])
            send[slot(0, k, t)] = (weight * g).astype(BF16)
        return carry

    lax.fori_loop(0, tokens, token, 0, unroll=4)
    fetch(send, sent, sems.at[0]).wait()


def finish_kernel(own_slots, other_slots, back, upstream, out, away, keep, low, up, sems):
    tokens, depth = upstream.shape[0], upstream.shape[1]
    upper = on_core(1)
    slot = slot_reader(own_slots, other_slots)

    def token(t, carry):
        at = pl.ds(pl.multiple_of(t * depth, depth), depth)
        g = upstream[t].astype(F32)
        up[at, :] = g
        total = g
        for k in range(2):
            total = total + back[slot(0, k, t)].astype(F32)
        low[at, :] = total
        return carry

    lax.fori_loop(0, tokens, token, 0, unroll=4)
    for j in range(depth):
        columns = slice(j * LANES, (j + 1) * LANES)
        high = up[pl.ds(j, tokens, stride=depth), :]
        down = low[pl.ds(j, tokens, stride=depth), :]
        keep[:, columns] = jnp.where(upper, high, down).astype(BF16)
        away[:, columns] = jnp.where(upper, down, high).astype(BF16)
    fetch(keep, out.at[lax.axis_index("segment")], sems.at[0]).wait()


def join_kernel(came, partial, out, sems):
    fetch(came, out.at[1 - lax.axis_index("segment")], sems.at[0]).wait()


def turn_kernel(turn, gate, up, down, *refs):
    gate_up_t, down_t, a, b, c, turned, turned_down, sems = refs[-8:]
    hidden, width = down.shape
    step = 256

    def work():
        copies = [
            fetch(gate, a, sems.at[0]), fetch(up, b, sems.at[1]), fetch(down, c, sems.at[2])
        ]
        for n, block in enumerate((a, b)):
            copies[n].wait()
            for i in range(0, width, step):
                turned[n * hidden : (n + 1) * hidden, i : i + step] = block[i : i + step, :].T
        first = fetch(turned, gate_up_t, sems.at[3])
        copies[2].wait()
        for i in range(0, width, step):
            turned_down[i : i + step, :] = c[:, i : i + step].T
        fetch(turned_down, down_t, sems.at[4]).wait()
        first.wait()

    if turn is None:
        work()
    else:
        pl.when(on_core(turn))(work)


def forward_parts(rows, gate, up):
    hidden_gate = jnp.dot(rows[...], gate[...], preferred_element_type=F32)
    hidden_up = jnp.dot(rows[...], up[...], preferred_element_type=F32)
    sigma = 1.0 / (1.0 + jnp.exp(-hidden_gate))
    act = hidden_gate * sigma
    dact = sigma * (1.0 + hidden_gate * (1.0 - sigma))
    return act, hidden_up * dact, (act * hidden_up).astype(BF16)


def back_part(grad_act, act, slope, gate_up_t, tiles, send, sent, sems):
    count, depth, lanes = send.shape
    both = jnp.concatenate(
        [(grad_act * slope).astype(BF16), (grad_act * act).astype(BF16)], axis=1
    )
    dx = jnp.dot(both, gate_up_t[...], preferred_element_type=F32)
    rows_to_tiles(dx, tiles, count, depth)
    pieces, copies = 4, []
    part = count // pieces
    for n in range(pieces):
        rows = tiles[n * part * depth : (n + 1) * part * depth, :]
        send[n * part : (n + 1) * part] = rows.reshape(part, depth, lanes).astype(BF16)
        here = pl.ds(n * part, part)
        copies.append(fetch(send.at[here], sent.at[here], sems.at[n]))
    return copies


def untile(block, tiles, rows, depth):
    count = rows.shape[0]
    tiles[...] = block.astype(F32).reshape(count * depth, LANES)
    tiles_to_rows(tiles, rows, count, depth)


def upper_kernel(
    arrived, own_gate, other_gate, own_up, other_up, own_dt, other_dt, own_gut, other_gut, after,
    sent, dy_out, act_out,
    gate, up, down_t, gate_up_t, tiles, x_rows, dy_rows, activ, send, sems,
):
    mine = on_core(1)
    depth = send.shape[1]
    gate_copy = fetch_one_of(mine, own_gate, other_gate, gate, sems.at[0])
    up_copy = fetch_one_of(mine, own_up, other_up, up, sems.at[1])
    down_copy = fetch_one_of(mine, own_dt, other_dt, down_t, sems.at[2])
    back_copy = fetch_one_of(mine, own_gut, other_gut, gate_up_t, sems.at[3])
    untile(arrived[:, :CAP], tiles, x_rows, depth)
    gate_copy.wait()
    up_copy.wait()
    act, slope, rounded = forward_parts(x_rows, gate, up)
    activ[...] = rounded
    untile(arrived[:, CAP : 2 * CAP], tiles, dy_rows, depth)
    saves = [fetch(activ, act_out, sems.at[4]), fetch(dy_rows, dy_out, sems.at[5])]
    down_copy.wait()
    grad_act = jnp.dot(dy_rows[...], down_t[...], preferred_element_type=F32)
    back_copy.wait()
    saves += back_part(grad_act, act, slope, gate_up_t, tiles, send, sent, sems.at[pl.ds(6, 4)])
    for copy in saves:
        copy.wait()


def forward_kernel(core, arrived, matrix_gate, matrix_up, *refs):
    act_out, slope_out, activ_out, act, slope, activ, gate, up, tiles, x_rows, sems = refs[-11:]
    depth = arrived.shape[2]

    def work():
        gate_copy = fetch(matrix_gate, gate, sems.at[0])
        up_copy = fetch(matrix_up, up, sems.at[1])
        untile(arrived[:, 2 * CAP :], tiles, x_rows, depth)
        gate_copy.wait()
        up_copy.wait()
        act[...], slope[...], activ[...] = forward_parts(x_rows, gate, up)
        saves = [
            fetch(act, act_out, sems.at[2]),
            fetch(slope, slope_out, sems.at[3]),
            fetch(activ, activ_out, sems.at[4]),
        ]
        for copy in saves:
            copy.wait()

    pl.when(on_core(core))(work)


def lower_kernel(
    dy, act_in, slope_in, own_dt, other_dt, own_gut, other_gut, sent, dy_out,
    act, slope, down_t, gate_up_t, tiles, dy_rows, send, sems,
):
    mine = on_core(0)
    down_copy = fetch_one_of(mine, own_dt, other_dt, down_t, sems.at[0])
    act_copy = fetch(act_in, act, sems.at[1])
    slope_copy = fetch(slope_in, slope, sems.at[2])
    back_copy = fetch_one_of(mine, own_gut, other_gut, gate_up_t, sems.at[3])
    untile(dy[...], tiles, dy_rows, send.shape[1])
    saves = [fetch(dy_rows, dy_out, sems.at[4])]
    down_copy.wait()
    grad_act = jnp.dot(dy_rows[...], down_t[...], preferred_element_type=F32)
    for copy in (act_copy, slope_copy, back_copy):
        copy.wait()
    saves += back_part(
        grad_act, act[...], slope[...], gate_up_t, tiles, send, sent, sems.at[pl.ds(5, 4)]
    )
    for copy in saves:
        copy.wait()


INPLACE = pl.BlockSpec(memory_space=pltpu.VMEM)


def placed(arg, spec):
    if spec is HBM:
        return pltpu.with_memory_space_constraint(arg, pltpu.HBM)
    if spec is INPLACE:
        return pltpu.with_memory_space_constraint(arg, pltpu.VMEM)
    return arg


def call(kernel, args, in_specs, out_shape, out_specs, scratch, flops, moved, aliases={}):
    return pl.pallas_call(
        kernel,
        in_specs=in_specs,
        out_shape=tuple(
            pltpu.HBM(out.shape, out.dtype) if spec is HBM else out
            for out, spec in zip(out_shape, out_specs)
        ),
        out_specs=out_specs,
        scratch_shapes=scratch,
        input_output_aliases=aliases,
        compiler_params=pltpu.CompilerParams(vmem_limit_bytes=VMEM_MIB * 1024 * 1024),
        cost_estimate=pl.CostEstimate(flops=flops, bytes_accessed=moved, transcendentals=0),
    )(*[placed(arg, spec) for arg, spec in zip(args, in_specs)])


def swapped(block):
    return lax.ppermute(block, "segment", [(0, 1), (1, 0)])


def exchanged(block):
    return lax.all_to_all(block, "expert", split_axis=0, concat_axis=0, tiled=True)


def shape(dims, kind=BF16):
    return jax.ShapeDtypeStruct(dims, kind)


def shards(saved_input, out_grad, expert_ids, router_weights, w_gate, w_up, w_down, eigenbasis):
    experts = lax.axis_size("expert")
    segment = lax.axis_index("segment")
    upper = segment == 1
    micros, tokens, width = saved_input.shape[1:]
    hidden = w_gate.shape[-1]
    depth = width // LANES
    count = experts * CAP
    gate, up, down, basis = w_gate[0, 0], w_up[0, 0], w_down[0, 0], eigenbasis[0, 0]

    other_x = swapped(
        lax.dynamic_index_in_dim(saved_input[0], 1 - segment, 0, keepdims=False)
    )
    ids = jnp.swapaxes(expert_ids[0], 1, 2)
    own_w = jnp.swapaxes(router_weights[0], 1, 2)
    order = 2 * np.arange(tokens)[None, :] + np.arange(2)[:, None]
    earlier = order[None, None] < order[..., None, None]
    same = ids[:, None, None] == ids[..., None, None]
    rank = jnp.sum((same & earlier[None]).astype(jnp.int32), axis=(3, 4))
    own_slots = ids * CAP + jnp.minimum(rank, CAP - 1)
    other_slots, other_w = swapped(own_slots), swapped(own_w)

    matrix = pltpu.VMEM((width, hidden), BF16)
    turned_shapes = (shape((2 * hidden, width)), shape((width, hidden)))
    turn_scratch = [
        matrix, matrix, pltpu.VMEM((hidden, width), BF16), pltpu.VMEM((2 * hidden, width), BF16),
        matrix, pltpu.SemaphoreType.DMA((5,)),
    ]

    def turned(turn, matrices, made=()):
        return call(
            functools.partial(turn_kernel, turn),
            (*matrices, *made),
            [HBM] * (3 + len(made)),
            turned_shapes,
            (HBM,) * 2,
            turn_scratch,
            1_000_000,
            9_000_000,
            {3: 0, 4: 1} if made else {},
        )

    early_gut, early_dt = turned(0, (gate, up, down))

    tile_rows = tokens * depth
    row_block = pltpu.VMEM((tokens, width), BF16)
    send, grad_tiles = call(
        dispatch_kernel,
        (own_slots, other_slots, own_w, other_w, saved_input[0], other_x, out_grad, early_dt),
        [SMEM] * 4 + [HBM] * 4,
        (shape((experts, 3 * CAP, depth, LANES)), shape((tokens, depth, LANES))),
        (HBM,) * 2,
        [
            pltpu.VMEM((experts, 3 * CAP, depth, LANES), BF16),
            pltpu.VMEM((tokens, depth, LANES), BF16),
        ]
        + [row_block] * 3
        + [pltpu.VMEM((tile_rows, LANES), F32)] * 3
        + [pltpu.SemaphoreType.DMA((7,))],
        1_000_000,
        5_000_000,
    )
    arrived = exchanged(send)

    own_gut, own_dt = turned(1, (gate, up, down), (early_gut, early_dt))
    other_gate, other_up, other_down = swapped(gate), swapped(up), swapped(down)
    other_basis = swapped(basis)
    other_gut, other_dt = turned(None, (other_gate, other_up, other_down))

    tiles = pltpu.VMEM((count * depth, LANES), F32)
    rows = pltpu.VMEM((count, width), BF16)
    flat = (count, depth, LANES)
    flat_scratch = pltpu.VMEM(flat, BF16)
    mat = 2 * count * width * hidden

    def forwarded(core, matrix_gate, matrix_up, made=()):
        return call(
            functools.partial(forward_kernel, core),
            (arrived, matrix_gate, matrix_up, *made),
            [INPLACE] + [HBM] * (2 + len(made)),
            (shape((count, hidden), F32), shape((count, hidden), F32), shape((count, hidden))),
            (HBM,) * 3,
            [
                pltpu.VMEM((count, hidden), F32), pltpu.VMEM((count, hidden), F32),
                pltpu.VMEM((count, hidden), BF16), matrix, matrix, tiles, rows,
                pltpu.SemaphoreType.DMA((5,)),
            ],
            2 * mat,
            5_000_000,
            {3 + n: n for n in range(len(made))},
        )

    early = forwarded(0, gate, up)
    back_send, dy_rows1, activ1 = call(
        upper_kernel,
        (
            arrived, gate, other_gate, up, other_up, own_dt, other_dt, own_gut, other_gut,
            early[2],
        ),
        [INPLACE] + [HBM] * 9,
        (shape(flat), shape((count, width)), shape((count, hidden))),
        (HBM,) * 3,
        [
            matrix, matrix, matrix, pltpu.VMEM((2 * hidden, width), BF16), tiles,
            rows, rows, pltpu.VMEM((count, hidden), BF16), flat_scratch,
            pltpu.SemaphoreType.DMA((10,)),
        ],
        5 * mat,
        9_000_000,
    )

    def returned(block):
        return exchanged(block.reshape(experts, CAP, depth, LANES)).reshape(flat)

    back = returned(back_send)
    act0, slope0, activ0 = forwarded(1, other_gate, other_up, early)
    basis1 = jnp.where(upper, basis, other_basis)
    basis0 = jnp.where(upper, other_basis, basis)
    rotated1 = jnp.dot(activ1, basis1, preferred_element_type=F32).astype(BF16)
    rotated0 = jnp.dot(activ0, basis0, preferred_element_type=F32).astype(BF16)

    dy_send, grad1 = call(
        relay_kernel,
        (own_slots, other_slots, own_w, other_w, back, grad_tiles),
        [SMEM] * 4 + [INPLACE, VMEM],
        (shape(flat), shape((tokens, depth, LANES))),
        (HBM, VMEM),
        [flat_scratch, pltpu.SemaphoreType.DMA((1,))],
        1_000_000,
        3_000_000,
    )
    dy = returned(dy_send)
    back_send0, dy_rows0 = call(
        lower_kernel,
        (dy, act0, slope0, own_dt, other_dt, own_gut, other_gut),
        [INPLACE] + [HBM] * 6,
        (shape(flat), shape((count, width))),
        (HBM,) * 2,
        [
            pltpu.VMEM((count, hidden), F32), pltpu.VMEM((count, hidden), F32),
            matrix, pltpu.VMEM((2 * hidden, width), BF16), tiles, rows, flat_scratch,
            pltpu.SemaphoreType.DMA((9,)),
        ],
        3 * mat,
        8_000_000,
    )
    back0 = returned(back_send0)

    all_rotated = jnp.concatenate(
        [
            jnp.where(upper, rotated1, rotated0),
            swapped(jnp.where(upper, rotated0, rotated1)),
        ],
        axis=0,
    )
    all_dy = jnp.concatenate(
        [
            jnp.where(upper, dy_rows1, dy_rows0),
            swapped(jnp.where(upper, dy_rows0, dy_rows1)),
        ],
        axis=0,
    )
    rot_sq = (all_rotated.astype(F32) ** 2).astype(BF16)
    dy_sq = (all_dy.astype(F32) ** 2).astype(BF16)
    over_rows = (((0,), (0,)), ((), ()))
    grad_sum = lax.dot_general(all_rotated, all_dy, over_rows, preferred_element_type=F32)
    scale_sum = lax.dot_general(rot_sq, dy_sq, over_rows, preferred_element_type=F32)
    rotated_grad = (grad_sum * (1.0 / micros)).astype(BF16)
    ekfac_scales = scale_sum * (1.0 / micros)
    back0, rotated_grad, ekfac_scales = lax.optimization_barrier(
        (back0, rotated_grad, ekfac_scales)
    )

    own_grads, away = call(
        finish_kernel,
        (own_slots, other_slots, back0, grad1),
        [SMEM] * 2 + [INPLACE, VMEM],
        (shape((micros, tokens, width)), shape((tokens, width))),
        (HBM, VMEM),
        [row_block]
        + [pltpu.VMEM((tile_rows, LANES), F32)] * 2
        + [pltpu.SemaphoreType.DMA((1,))],
        1_000_000,
        2_000_000,
    )
    (grads,) = call(
        join_kernel,
        (swapped(away), own_grads),
        [INPLACE, HBM],
        (shape((micros, tokens, width)),),
        (HBM,),
        [pltpu.SemaphoreType.DMA((1,))],
        0,
        1_000_000,
        {1: 0},
    )
    return (grads[None], rotated_grad[None, None], ekfac_scales[None, None])


def solution(mesh):
    in_specs = (
        P("segment", None, "expert", None),
        P(None, "expert", None),
        P("segment", None, "expert", None),
        P("segment", None, "expert", None),
        P("segment", "expert", None, None),
        P("segment", "expert", None, None),
        P("segment", "expert", None, None),
        P("segment", "expert", None, None),
    )
    out_specs = (
        P("segment", None, "expert", None),
        P("segment", "expert", None, None),
        P("segment", "expert", None, None),
    )
    return jax.shard_map(shards, mesh=mesh, in_specs=in_specs, out_specs=out_specs, check_vma=False)
```

```python
import functools
import jax
import jax.numpy as jnp
import numpy as np
from jax import lax
from jax.experimental import pallas as pl
from jax.experimental.pallas import tpu as pltpu
from jax.sharding import PartitionSpec as P

LANES = 128
CAP = 2
F32 = jnp.float32
BF16 = jnp.bfloat16
SMEM = pl.BlockSpec(memory_space=pltpu.SMEM)
VMEM = pl.BlockSpec(memory_space=pltpu.VMEM)
HBM = pl.BlockSpec(memory_space=pltpu.HBM)
VMEM_MIB = 28


def rows_to_tiles(rows, tiles, count, depth):
    for j in range(depth):
        tiles[pl.ds(j, count, stride=depth), :] = rows[:, j * LANES : (j + 1) * LANES]


def tiles_to_rows(tiles, rows, count, depth):
    for j in range(depth):
        rows[:, j * LANES : (j + 1) * LANES] = tiles[pl.ds(j, count, stride=depth), :].astype(
            rows.dtype
        )


def clear(send, experts):
    zero = jnp.zeros(send.shape[1:], send.dtype)

    def one(e, carry):
        send[e] = zero
        return carry

    lax.fori_loop(0, experts, one, 0, unroll=8)


def on_core(which):
    return lax.axis_index("segment") == which


def fetch(source, target, sem):
    copy = pltpu.make_async_copy(source, target, sem)
    copy.start()
    return copy


def fetch_one_of(first, own, other, target, sem):
    @pl.when(first)
    def _():
        pltpu.make_async_copy(own, target, sem).start()

    @pl.when(jnp.logical_not(first))
    def _():
        pltpu.make_async_copy(other, target, sem).start()

    return pltpu.make_async_copy(own, target, sem)


def slot_reader(own_slots, other_slots):
    segment = lax.axis_index("segment")

    def slot(layer, k, t):
        mine, theirs = own_slots[segment, k, t], other_slots[segment, k, t]
        return jnp.where(segment == layer, mine, theirs)

    return slot


def dispatch_kernel(
    own_slots, other_slots, own_w, other_w, own_x, other_x, grads, after, sent, tiles_out,
    send, grad_tiles, own, grad, x_upper, x_lower, g_tiles, sems,
):
    tokens, width = grad.shape
    depth = width // LANES
    segment = lax.axis_index("segment")
    upper = segment == 1
    slot = slot_reader(own_slots, other_slots)
    copies = [
        fetch(own_x.at[segment], own, sems.at[0]),
        fetch(grads.at[segment], grad, sems.at[2]),
    ]
    clear(send, send.shape[0])
    for copy in copies:
        copy.wait()
    mine, theirs = own[...].astype(F32), other_x[...].astype(F32)
    rows_to_tiles(jnp.where(upper, mine, theirs), x_upper, tokens, depth)
    saves = []

    def part(n):
        here = slice(n * CAP, (n + 1) * CAP)
        saves.append(fetch(send.at[:, here], sent.at[:, here], sems.at[3 + n]))

    def first(t, carry):
        row = x_upper[pl.ds(pl.multiple_of(t * depth, depth), depth), :].astype(BF16)
        for k in range(2):
            s = slot(1, k, t)
            send[s >> 1, s & 1] = row
        return carry

    lax.fori_loop(0, tokens, first, 0, unroll=4)
    part(0)
    rows_to_tiles(grad[...].astype(F32), g_tiles, tokens, depth)

    def second(t, carry):
        g = g_tiles[pl.ds(pl.multiple_of(t * depth, depth), depth), :]
        grad_tiles[t] = g.astype(BF16)
        for k in range(2):
            s = slot(1, k, t)
            weight = jnp.where(upper, own_w[segment, k, t], other_w[segment, k, t])
            send[s >> 1, CAP + (s & 1)] = (weight * g).astype(BF16)
        return carry

    lax.fori_loop(0, tokens, second, 0, unroll=4)
    part(1)
    saves.append(fetch(grad_tiles, tiles_out, sems.at[6]))
    rows_to_tiles(jnp.where(upper, theirs, mine), x_lower, tokens, depth)

    def third(t, carry):
        row = x_lower[pl.ds(pl.multiple_of(t * depth, depth), depth), :].astype(BF16)
        for k in range(2):
            s = slot(0, k, t)
            send[s >> 1, 2 * CAP + (s & 1)] = row
        return carry

    lax.fori_loop(0, tokens, third, 0, unroll=4)
    part(2)
    for copy in saves:
        copy.wait()


def relay_kernel(
    own_slots, other_slots, own_w, other_w, back, upstream, sent, grad_out, send, grads, sems
):
    tokens = upstream.shape[0]
    segment = lax.axis_index("segment")
    upper = segment == 1
    slot = slot_reader(own_slots, other_slots)
    clear(send, send.shape[0])

    def token(t, carry):
        total = upstream[t].astype(F32)
        for k in range(2):
            total = total + back[slot(1, k, t)].astype(F32)
        rounded = total.astype(BF16)
        grads[t] = rounded
        g = rounded.astype(F32)
        for k in range(2):
            weight = jnp.where(upper, other_w[segment, k, t], own_w[segment, k, t])
            send[slot(0, k, t)] = (weight * g).astype(BF16)
        return carry

    lax.fori_loop(0, tokens, token, 0, unroll=4)
    saves = [fetch(send, sent, sems.at[0]), fetch(grads, grad_out, sems.at[1])]
    for copy in saves:
        copy.wait()


def stow_kernel(upstream, out, away, block, tiles, rows, sems):
    tokens, depth = block.shape[:2]
    fetch(upstream, block, sems.at[0]).wait()
    tiles[...] = block[...].astype(F32).reshape(tiles.shape)
    tiles_to_rows(tiles, rows, tokens, depth)

    @pl.when(on_core(1))
    def _():
        fetch(rows, out.at[1], sems.at[1]).wait()

    @pl.when(on_core(0))
    def _():
        fetch(rows, away, sems.at[1]).wait()


def finish_kernel(core, own_in, other_in, back, upstream, made, out, *scratch):
    own_slots, other_slots, block, tiles, rows, sems = scratch
    tokens, depth = block.shape[:2]

    def work():
        copies = [
            fetch(own_in, own_slots, sems.at[0]),
            fetch(other_in, other_slots, sems.at[1]),
            fetch(upstream, block, sems.at[2]),
        ]
        for copy in copies:
            copy.wait()
        slots = own_slots if core == 0 else other_slots

        def token(t, carry):
            total = block[t].astype(F32)
            for k in range(2):
                total = total + back[slots[core, k, t]].astype(F32)
            tiles[pl.ds(pl.multiple_of(t * depth, depth), depth), :] = total
            return carry

        lax.fori_loop(0, tokens, token, 0, unroll=4)
        tiles_to_rows(tiles, rows, tokens, depth)
        fetch(rows, out if core == 1 else out.at[0], sems.at[3]).wait()

    pl.when(on_core(core))(work)


def join_kernel(came, partial, out, sems):
    fetch(came, out.at[1 - lax.axis_index("segment")], sems.at[0]).wait()


def turn_kernel(turn, gate, up, down, *refs):
    gate_up_t, down_t, a, b, c, turned, turned_down, sems = refs[-8:]
    hidden, width = down.shape
    step = 256

    def work():
        copies = [
            fetch(gate, a, sems.at[0]), fetch(up, b, sems.at[1]), fetch(down, c, sems.at[2])
        ]
        for n, block in enumerate((a, b)):
            copies[n].wait()
            for i in range(0, width, step):
                turned[n * hidden : (n + 1) * hidden, i : i + step] = block[i : i + step, :].T
        first = fetch(turned, gate_up_t, sems.at[3])
        copies[2].wait()
        for i in range(0, width, step):
            turned_down[i : i + step, :] = c[:, i : i + step].T
        fetch(turned_down, down_t, sems.at[4]).wait()
        first.wait()

    if turn is None:
        work()
    else:
        pl.when(on_core(turn))(work)


def forward_parts(rows, gate, up):
    hidden_gate = jnp.dot(rows[...], gate[...], preferred_element_type=F32)
    hidden_up = jnp.dot(rows[...], up[...], preferred_element_type=F32)
    sigma = 1.0 / (1.0 + jnp.exp(-hidden_gate))
    act = hidden_gate * sigma
    dact = sigma * (1.0 + hidden_gate * (1.0 - sigma))
    return act, hidden_up * dact, (act * hidden_up).astype(BF16)


def back_part(grad_act, act, slope, gate_up_t, tiles, send, sent, sems):
    count, depth, lanes = send.shape
    both = jnp.concatenate(
        [(grad_act * slope).astype(BF16), (grad_act * act).astype(BF16)], axis=1
    )
    dx = jnp.dot(both, gate_up_t[...], preferred_element_type=F32)
    rows_to_tiles(dx, tiles, count, depth)
    pieces, copies = 4, []
    part = count // pieces
    for n in range(pieces):
        rows = tiles[n * part * depth : (n + 1) * part * depth, :]
        send[n * part : (n + 1) * part] = rows.reshape(part, depth, lanes).astype(BF16)
        here = pl.ds(n * part, part)
        copies.append(fetch(send.at[here], sent.at[here], sems.at[n]))
    return copies


def untile(block, tiles, rows, depth):
    count = rows.shape[0]
    tiles[...] = block.astype(F32).reshape(count * depth, LANES)
    tiles_to_rows(tiles, rows, count, depth)


def upper_kernel(
    arrived, own_gate, other_gate, own_up, other_up, own_dt, other_dt, own_gut, other_gut, after,
    sent, dy_out, act_out,
    gate, up, down_t, gate_up_t, tiles, x_rows, dy_rows, activ, send, sems,
):
    mine = on_core(1)
    depth = send.shape[1]
    gate_copy = fetch_one_of(mine, own_gate, other_gate, gate, sems.at[0])
    up_copy = fetch_one_of(mine, own_up, other_up, up, sems.at[1])
    down_copy = fetch_one_of(mine, own_dt, other_dt, down_t, sems.at[2])
    back_copy = fetch_one_of(mine, own_gut, other_gut, gate_up_t, sems.at[3])
    untile(arrived[:, :CAP], tiles, x_rows, depth)
    gate_copy.wait()
    up_copy.wait()
    act, slope, rounded = forward_parts(x_rows, gate, up)
    activ[...] = rounded
    untile(arrived[:, CAP : 2 * CAP], tiles, dy_rows, depth)
    saves = [fetch(activ, act_out, sems.at[4]), fetch(dy_rows, dy_out, sems.at[5])]
    down_copy.wait()
    grad_act = jnp.dot(dy_rows[...], down_t[...], preferred_element_type=F32)
    back_copy.wait()
    saves += back_part(grad_act, act, slope, gate_up_t, tiles, send, sent, sems.at[pl.ds(6, 4)])
    for copy in saves:
        copy.wait()


def forward_kernel(core, arrived, matrix_gate, matrix_up, *refs):
    act_out, slope_out, activ_out, act, slope, activ, gate, up, tiles, x_rows, sems = refs[-11:]
    depth = arrived.shape[2]

    def work():
        gate_copy = fetch(matrix_gate, gate, sems.at[0])
        up_copy = fetch(matrix_up, up, sems.at[1])
        untile(arrived[:, 2 * CAP :], tiles, x_rows, depth)
        gate_copy.wait()
        up_copy.wait()
        act[...], slope[...], activ[...] = forward_parts(x_rows, gate, up)
        saves = [
            fetch(act, act_out, sems.at[2]),
            fetch(slope, slope_out, sems.at[3]),
            fetch(activ, activ_out, sems.at[4]),
        ]
        for copy in saves:
            copy.wait()

    pl.when(on_core(core))(work)


def lower_kernel(
    dy_in, act_in, slope_in, own_dt, other_dt, own_gut, other_gut, sent, dy_out,
    dy, act, slope, down_t, gate_up_t, tiles, dy_rows, send, sems,
):
    mine = on_core(0)
    count, depth = send.shape[:2]
    pieces = 4
    part = count // pieces
    arriving = [
        fetch(dy_in.at[pl.ds(n * part, part)], dy.at[pl.ds(n * part, part)], sems.at[9 + n])
        for n in range(pieces)
    ]
    down_copy = fetch_one_of(mine, own_dt, other_dt, down_t, sems.at[0])
    act_copy = fetch(act_in, act, sems.at[1])
    slope_copy = fetch(slope_in, slope, sems.at[2])
    back_copy = fetch_one_of(mine, own_gut, other_gut, gate_up_t, sems.at[3])
    for n, copy in enumerate(arriving):
        copy.wait()
        tiles[n * part * depth : (n + 1) * part * depth, :] = (
            dy[n * part : (n + 1) * part].astype(F32).reshape(part * depth, LANES)
        )
    tiles_to_rows(tiles, dy_rows, count, depth)
    saves = [fetch(dy_rows, dy_out, sems.at[4])]
    down_copy.wait()
    grad_act = jnp.dot(dy_rows[...], down_t[...], preferred_element_type=F32)
    for copy in (act_copy, slope_copy, back_copy):
        copy.wait()
    saves += back_part(
        grad_act, act[...], slope[...], gate_up_t, tiles, send, sent, sems.at[pl.ds(5, 4)]
    )
    for copy in saves:
        copy.wait()


INPLACE = pl.BlockSpec(memory_space=pltpu.VMEM)


def placed(arg, spec):
    if spec is HBM:
        return pltpu.with_memory_space_constraint(arg, pltpu.HBM)
    if spec is INPLACE:
        return pltpu.with_memory_space_constraint(arg, pltpu.VMEM)
    return arg


def call(kernel, args, in_specs, out_shape, out_specs, scratch, flops, moved, aliases={}):
    return pl.pallas_call(
        kernel,
        in_specs=in_specs,
        out_shape=tuple(
            pltpu.HBM(out.shape, out.dtype) if spec is HBM else out
            for out, spec in zip(out_shape, out_specs)
        ),
        out_specs=out_specs,
        scratch_shapes=scratch,
        input_output_aliases=aliases,
        compiler_params=pltpu.CompilerParams(vmem_limit_bytes=VMEM_MIB * 1024 * 1024),
        cost_estimate=pl.CostEstimate(flops=flops, bytes_accessed=moved, transcendentals=0),
    )(*[placed(arg, spec) for arg, spec in zip(args, in_specs)])


def swapped(block):
    return lax.ppermute(block, "segment", [(0, 1), (1, 0)])


def exchanged(block):
    return lax.all_to_all(block, "expert", split_axis=0, concat_axis=0, tiled=True)


def shape(dims, kind=BF16):
    return jax.ShapeDtypeStruct(dims, kind)


def shards(saved_input, out_grad, expert_ids, router_weights, w_gate, w_up, w_down, eigenbasis):
    experts = lax.axis_size("expert")
    segment = lax.axis_index("segment")
    upper = segment == 1
    micros, tokens, width = saved_input.shape[1:]
    hidden = w_gate.shape[-1]
    depth = width // LANES
    count = experts * CAP
    gate, up, down, basis = w_gate[0, 0], w_up[0, 0], w_down[0, 0], eigenbasis[0, 0]

    other_x = swapped(
        lax.dynamic_index_in_dim(saved_input[0], 1 - segment, 0, keepdims=False)
    )
    ids = jnp.swapaxes(expert_ids[0], 1, 2)
    own_w = jnp.swapaxes(router_weights[0], 1, 2)
    order = 2 * np.arange(tokens)[None, :] + np.arange(2)[:, None]
    earlier = order[None, None] < order[..., None, None]
    same = ids[:, None, None] == ids[..., None, None]
    rank = jnp.sum((same & earlier[None]).astype(jnp.int32), axis=(3, 4))
    own_slots = ids * CAP + jnp.minimum(rank, CAP - 1)
    other_slots, other_w = swapped(own_slots), swapped(own_w)

    matrix = pltpu.VMEM((width, hidden), BF16)
    turned_shapes = (shape((2 * hidden, width)), shape((width, hidden)))
    turn_scratch = [
        matrix, matrix, pltpu.VMEM((hidden, width), BF16), pltpu.VMEM((2 * hidden, width), BF16),
        matrix, pltpu.SemaphoreType.DMA((5,)),
    ]

    def turned(turn, matrices, made=()):
        return call(
            functools.partial(turn_kernel, turn),
            (*matrices, *made),
            [HBM] * (3 + len(made)),
            turned_shapes,
            (HBM,) * 2,
            turn_scratch,
            1_000_000,
            9_000_000,
            {3: 0, 4: 1} if made else {},
        )

    early_gut, early_dt = turned(0, (gate, up, down))

    tile_rows = tokens * depth
    row_block = pltpu.VMEM((tokens, width), BF16)
    send, grad_tiles = call(
        dispatch_kernel,
        (own_slots, other_slots, own_w, other_w, saved_input[0], other_x, out_grad, early_dt),
        [SMEM] * 4 + [HBM, INPLACE, HBM, HBM],
        (shape((experts, 3 * CAP, depth, LANES)), shape((tokens, depth, LANES))),
        (HBM,) * 2,
        [
            pltpu.VMEM((experts, 3 * CAP, depth, LANES), BF16),
            pltpu.VMEM((tokens, depth, LANES), BF16),
        ]
        + [row_block] * 2
        + [pltpu.VMEM((tile_rows, LANES), F32)] * 3
        + [pltpu.SemaphoreType.DMA((7,))],
        1_000_000,
        5_000_000,
    )
    arrived = exchanged(send)

    own_gut, own_dt = turned(1, (gate, up, down), (early_gut, early_dt))
    other_gate, other_up, other_down = swapped(gate), swapped(up), swapped(down)
    other_basis = swapped(basis)
    other_gut, other_dt = turned(None, (other_gate, other_up, other_down))

    tiles = pltpu.VMEM((count * depth, LANES), F32)
    rows = pltpu.VMEM((count, width), BF16)
    flat = (count, depth, LANES)
    flat_scratch = pltpu.VMEM(flat, BF16)
    mat = 2 * count * width * hidden

    def forwarded(core, matrix_gate, matrix_up, made=()):
        return call(
            functools.partial(forward_kernel, core),
            (arrived, matrix_gate, matrix_up, *made),
            [INPLACE] + [HBM] * (2 + len(made)),
            (shape((count, hidden), F32), shape((count, hidden), F32), shape((count, hidden))),
            (HBM,) * 3,
            [
                pltpu.VMEM((count, hidden), F32), pltpu.VMEM((count, hidden), F32),
                pltpu.VMEM((count, hidden), BF16), matrix, matrix, tiles, rows,
                pltpu.SemaphoreType.DMA((5,)),
            ],
            2 * mat,
            5_000_000,
            {3 + n: n for n in range(len(made))},
        )

    early = forwarded(0, gate, up)
    back_send, dy_rows1, activ1 = call(
        upper_kernel,
        (
            arrived, gate, other_gate, up, other_up, own_dt, other_dt, own_gut, other_gut,
            early[2],
        ),
        [INPLACE] + [HBM] * 9,
        (shape(flat), shape((count, width)), shape((count, hidden))),
        (HBM,) * 3,
        [
            matrix, matrix, matrix, pltpu.VMEM((2 * hidden, width), BF16), tiles,
            rows, rows, pltpu.VMEM((count, hidden), BF16), flat_scratch,
            pltpu.SemaphoreType.DMA((10,)),
        ],
        5 * mat,
        9_000_000,
    )

    def returned(block):
        return exchanged(block.reshape(experts, CAP, depth, LANES)).reshape(flat)

    back = returned(back_send)
    act0, slope0, activ0 = forwarded(1, other_gate, other_up, early)
    basis1 = jnp.where(upper, basis, other_basis)
    basis0 = jnp.where(upper, other_basis, basis)
    rotated1 = jnp.dot(activ1, basis1, preferred_element_type=F32).astype(BF16)
    rotated0 = jnp.dot(activ0, basis0, preferred_element_type=F32).astype(BF16)

    dy_send, grad1 = call(
        relay_kernel,
        (own_slots, other_slots, own_w, other_w, back, grad_tiles),
        [SMEM] * 4 + [INPLACE, VMEM],
        (shape(flat), shape((tokens, depth, LANES))),
        (HBM, HBM),
        [
            flat_scratch, pltpu.VMEM((tokens, depth, LANES), BF16),
            pltpu.SemaphoreType.DMA((2,)),
        ],
        1_000_000,
        3_000_000,
    )
    own_grads, away = call(
        stow_kernel,
        (grad1,),
        [HBM],
        (shape((micros, tokens, width)), shape((tokens, width))),
        (HBM,) * 2,
        [
            pltpu.VMEM((tokens, depth, LANES), BF16), pltpu.VMEM((tile_rows, LANES), F32),
            row_block, pltpu.SemaphoreType.DMA((2,)),
        ],
        1_000_000,
        1_000_000,
    )
    dy = returned(dy_send)
    back_send0, dy_rows0 = call(
        lower_kernel,
        (dy, act0, slope0, own_dt, other_dt, own_gut, other_gut),
        [HBM] * 7,
        (shape(flat), shape((count, width))),
        (HBM,) * 2,
        [
            flat_scratch, pltpu.VMEM((count, hidden), F32), pltpu.VMEM((count, hidden), F32),
            matrix, pltpu.VMEM((2 * hidden, width), BF16), tiles, rows, flat_scratch,
            pltpu.SemaphoreType.DMA((13,)),
        ],
        3 * mat,
        8_000_000,
    )
    back0 = returned(back_send0)

    all_rotated = jnp.concatenate(
        [
            jnp.where(upper, rotated1, rotated0),
            swapped(jnp.where(upper, rotated0, rotated1)),
        ],
        axis=0,
    )
    all_dy = jnp.concatenate(
        [
            jnp.where(upper, dy_rows1, dy_rows0),
            swapped(jnp.where(upper, dy_rows0, dy_rows1)),
        ],
        axis=0,
    )
    rot_sq = (all_rotated.astype(F32) ** 2).astype(BF16)
    dy_sq = (all_dy.astype(F32) ** 2).astype(BF16)
    over_rows = (((0,), (0,)), ((), ()))
    grad_sum = lax.dot_general(all_rotated, all_dy, over_rows, preferred_element_type=F32)
    scale_sum = lax.dot_general(rot_sq, dy_sq, over_rows, preferred_element_type=F32)
    rotated_grad = (grad_sum * (1.0 / micros)).astype(BF16)
    ekfac_scales = scale_sum * (1.0 / micros)
    back0, rotated_grad, ekfac_scales = lax.optimization_barrier(
        (back0, rotated_grad, ekfac_scales)
    )

    def finished(core, made):
        (out,) = call(
            functools.partial(finish_kernel, core),
            (own_slots, other_slots, back0, grad1, made),
            [HBM, HBM, INPLACE, HBM, HBM],
            (shape(made.shape),),
            (HBM,),
            [
                pltpu.SMEM((micros, 2, tokens), jnp.int32),
                pltpu.SMEM((micros, 2, tokens), jnp.int32),
                pltpu.VMEM((tokens, depth, LANES), BF16),
                pltpu.VMEM((tile_rows, LANES), F32),
                row_block,
                pltpu.SemaphoreType.DMA((4,)),
            ],
            3_000_000_000,
            2_000_000,
            {4: 0},
        )
        return out

    came = swapped(finished(1, away))
    own_grads = finished(0, own_grads)
    (grads,) = call(
        join_kernel,
        (came, own_grads),
        [INPLACE, HBM],
        (shape((micros, tokens, width)),),
        (HBM,),
        [pltpu.SemaphoreType.DMA((1,))],
        0,
        1_000_000,
        {1: 0},
    )
    return (grads[None], rotated_grad[None, None], ekfac_scales[None, None])


def solution(mesh):
    in_specs = (
        P("segment", None, "expert", None),
        P(None, "expert", None),
        P("segment", None, "expert", None),
        P("segment", None, "expert", None),
        P("segment", "expert", None, None),
        P("segment", "expert", None, None),
        P("segment", "expert", None, None),
        P("segment", "expert", None, None),
    )
    out_specs = (
        P("segment", None, "expert", None),
        P("segment", "expert", None, None),
        P("segment", "expert", None, None),
    )
    return jax.shard_map(shards, mesh=mesh, in_specs=in_specs, out_specs=out_specs, check_vma=False)
```

```python
import functools
import jax
import jax.numpy as jnp
import numpy as np
from jax import lax
from jax.experimental import pallas as pl
from jax.experimental.pallas import tpu as pltpu
from jax.sharding import PartitionSpec as P

LANES = 128
CAP = 2
F32 = jnp.float32
BF16 = jnp.bfloat16
SMEM = pl.BlockSpec(memory_space=pltpu.SMEM)
VMEM = pl.BlockSpec(memory_space=pltpu.VMEM)
HBM = pl.BlockSpec(memory_space=pltpu.HBM)
VMEM_MIB = 28


def rows_to_tiles(rows, tiles, count, depth):
    for j in range(depth):
        tiles[pl.ds(j, count, stride=depth), :] = rows[:, j * LANES : (j + 1) * LANES]


def tiles_to_rows(tiles, rows, count, depth):
    for j in range(depth):
        rows[:, j * LANES : (j + 1) * LANES] = tiles[pl.ds(j, count, stride=depth), :].astype(
            rows.dtype
        )


def clear(send, experts):
    zero = jnp.zeros(send.shape[1:], send.dtype)

    def one(e, carry):
        send[e] = zero
        return carry

    lax.fori_loop(0, experts, one, 0, unroll=8)


def on_core(which):
    return lax.axis_index("segment") == which


def fetch(source, target, sem):
    copy = pltpu.make_async_copy(source, target, sem)
    copy.start()
    return copy


def fetch_one_of(first, own, other, target, sem):
    @pl.when(first)
    def _():
        pltpu.make_async_copy(own, target, sem).start()

    @pl.when(jnp.logical_not(first))
    def _():
        pltpu.make_async_copy(other, target, sem).start()

    return pltpu.make_async_copy(own, target, sem)


def slot_reader(own_slots, other_slots):
    segment = lax.axis_index("segment")

    def slot(layer, k, t):
        mine, theirs = own_slots[segment, k, t], other_slots[segment, k, t]
        return jnp.where(segment == layer, mine, theirs)

    return slot


def dispatch_kernel(
    own_slots, other_slots, own_w, other_w, own_x, other_x, grads, after, sent, tiles_out,
    send, grad_tiles, own, grad, x_upper, x_lower, g_tiles, sems,
):
    tokens, width = grad.shape
    depth = width // LANES
    segment = lax.axis_index("segment")
    upper = segment == 1
    slot = slot_reader(own_slots, other_slots)
    copies = [
        fetch(own_x.at[segment], own, sems.at[0]),
        fetch(grads.at[segment], grad, sems.at[2]),
    ]
    clear(send, send.shape[0])
    for copy in copies:
        copy.wait()
    mine, theirs = own[...].astype(F32), other_x[...].astype(F32)
    rows_to_tiles(jnp.where(upper, mine, theirs), x_upper, tokens, depth)
    saves = []

    def part(n):
        here = slice(n * CAP, (n + 1) * CAP)
        saves.append(fetch(send.at[:, here], sent.at[:, here], sems.at[3 + n]))

    def first(t, carry):
        row = x_upper[pl.ds(pl.multiple_of(t * depth, depth), depth), :].astype(BF16)
        for k in range(2):
            s = slot(1, k, t)
            send[s >> 1, s & 1] = row
        return carry

    lax.fori_loop(0, tokens, first, 0, unroll=4)
    part(0)
    rows_to_tiles(grad[...].astype(F32), g_tiles, tokens, depth)

    def second(t, carry):
        g = g_tiles[pl.ds(pl.multiple_of(t * depth, depth), depth), :]
        grad_tiles[t] = g.astype(BF16)
        for k in range(2):
            s = slot(1, k, t)
            weight = jnp.where(upper, own_w[segment, k, t], other_w[segment, k, t])
            send[s >> 1, CAP + (s & 1)] = (weight * g).astype(BF16)
        return carry

    lax.fori_loop(0, tokens, second, 0, unroll=4)
    part(1)
    saves.append(fetch(grad_tiles, tiles_out, sems.at[6]))
    rows_to_tiles(jnp.where(upper, theirs, mine), x_lower, tokens, depth)

    def third(t, carry):
        row = x_lower[pl.ds(pl.multiple_of(t * depth, depth), depth), :].astype(BF16)
        for k in range(2):
            s = slot(0, k, t)
            send[s >> 1, 2 * CAP + (s & 1)] = row
        return carry

    lax.fori_loop(0, tokens, third, 0, unroll=4)
    part(2)
    for copy in saves:
        copy.wait()


def relay_kernel(
    own_slots, other_slots, own_w, other_w, back, upstream, sent, grad_out, send, grads, sems
):
    tokens = upstream.shape[0]
    segment = lax.axis_index("segment")
    upper = segment == 1
    slot = slot_reader(own_slots, other_slots)
    clear(send, send.shape[0])

    def token(t, carry):
        total = upstream[t].astype(F32)
        for k in range(2):
            total = total + back[slot(1, k, t)].astype(F32)
        rounded = total.astype(BF16)
        grads[t] = rounded
        g = rounded.astype(F32)
        for k in range(2):
            weight = jnp.where(upper, other_w[segment, k, t], own_w[segment, k, t])
            send[slot(0, k, t)] = (weight * g).astype(BF16)
        return carry

    lax.fori_loop(0, tokens, token, 0, unroll=8)
    saves = [fetch(send, sent, sems.at[0]), fetch(grads, grad_out, sems.at[1])]
    for copy in saves:
        copy.wait()


def stow_kernel(upstream, out, away, block, tiles, rows, sems):
    tokens, depth = block.shape[:2]
    fetch(upstream, block, sems.at[0]).wait()
    tiles[...] = block[...].astype(F32).reshape(tiles.shape)
    tiles_to_rows(tiles, rows, tokens, depth)

    @pl.when(on_core(1))
    def _():
        fetch(rows, out.at[1], sems.at[1]).wait()

    @pl.when(on_core(0))
    def _():
        fetch(rows, away, sems.at[1]).wait()


def finish_kernel(core, own_in, other_in, back, upstream, made, out, *scratch):
    own_slots, other_slots, block, tiles, rows, sems = scratch
    tokens, depth = block.shape[:2]

    def work():
        copies = [
            fetch(own_in, own_slots, sems.at[0]),
            fetch(other_in, other_slots, sems.at[1]),
            fetch(upstream, block, sems.at[2]),
        ]
        for copy in copies:
            copy.wait()
        slots = own_slots if core == 0 else other_slots

        def token(t, carry):
            total = block[t].astype(F32)
            for k in range(2):
                total = total + back[slots[core, k, t]].astype(F32)
            tiles[pl.ds(pl.multiple_of(t * depth, depth), depth), :] = total
            return carry

        lax.fori_loop(0, tokens, token, 0, unroll=4)
        tiles_to_rows(tiles, rows, tokens, depth)
        fetch(rows, out if core == 1 else out.at[0], sems.at[3]).wait()

    pl.when(on_core(core))(work)


def join_kernel(came, partial, out, sems):
    fetch(came, out.at[1 - lax.axis_index("segment")], sems.at[0]).wait()


def turn_kernel(turn, gate, up, down, *refs):
    gate_up_t, down_t, a, b, c, turned, turned_down, sems = refs[-8:]
    hidden, width = down.shape
    step = 256

    def work():
        copies = [
            fetch(gate, a, sems.at[0]), fetch(up, b, sems.at[1]), fetch(down, c, sems.at[2])
        ]
        for n, block in enumerate((a, b)):
            copies[n].wait()
            for i in range(0, width, step):
                turned[n * hidden : (n + 1) * hidden, i : i + step] = block[i : i + step, :].T
        first = fetch(turned, gate_up_t, sems.at[3])
        copies[2].wait()
        for i in range(0, width, step):
            turned_down[i : i + step, :] = c[:, i : i + step].T
        fetch(turned_down, down_t, sems.at[4]).wait()
        first.wait()

    if turn is None:
        work()
    else:
        pl.when(on_core(turn))(work)


def forward_parts(rows, gate, up):
    hidden_gate = jnp.dot(rows[...], gate[...], preferred_element_type=F32)
    hidden_up = jnp.dot(rows[...], up[...], preferred_element_type=F32)
    sigma = 1.0 / (1.0 + jnp.exp(-hidden_gate))
    act = hidden_gate * sigma
    dact = sigma * (1.0 + hidden_gate * (1.0 - sigma))
    return act, hidden_up * dact, (act * hidden_up).astype(BF16)


def back_part(grad_act, act, slope, gate_up_t, tiles, send, sent, sems):
    count, depth, lanes = send.shape
    both = jnp.concatenate(
        [(grad_act * slope).astype(BF16), (grad_act * act).astype(BF16)], axis=1
    )
    dx = jnp.dot(both, gate_up_t[...], preferred_element_type=F32)
    rows_to_tiles(dx, tiles, count, depth)
    pieces, copies = 4, []
    part = count // pieces
    for n in range(pieces):
        rows = tiles[n * part * depth : (n + 1) * part * depth, :]
        send[n * part : (n + 1) * part] = rows.reshape(part, depth, lanes).astype(BF16)
        here = pl.ds(n * part, part)
        copies.append(fetch(send.at[here], sent.at[here], sems.at[n]))
    return copies


def untile(block, tiles, rows, depth):
    count = rows.shape[0]
    tiles[...] = block.astype(F32).reshape(count * depth, LANES)
    tiles_to_rows(tiles, rows, count, depth)


def upper_kernel(
    arrived, own_gate, other_gate, own_up, other_up, own_dt, other_dt, own_gut, other_gut, after,
    sent, dy_out, act_out,
    gate, up, down_t, gate_up_t, tiles, x_rows, dy_rows, activ, send, sems,
):
    mine = on_core(1)
    depth = send.shape[1]
    gate_copy = fetch_one_of(mine, own_gate, other_gate, gate, sems.at[0])
    up_copy = fetch_one_of(mine, own_up, other_up, up, sems.at[1])
    untile(arrived[:, :CAP], tiles, x_rows, depth)
    gate_copy.wait()
    up_copy.wait()
    down_copy = fetch_one_of(mine, own_dt, other_dt, down_t, sems.at[2])
    back_copy = fetch_one_of(mine, own_gut, other_gut, gate_up_t, sems.at[3])
    act, slope, rounded = forward_parts(x_rows, gate, up)
    activ[...] = rounded
    untile(arrived[:, CAP : 2 * CAP], tiles, dy_rows, depth)
    saves = [fetch(activ, act_out, sems.at[4]), fetch(dy_rows, dy_out, sems.at[5])]
    down_copy.wait()
    grad_act = jnp.dot(dy_rows[...], down_t[...], preferred_element_type=F32)
    back_copy.wait()
    saves += back_part(grad_act, act, slope, gate_up_t, tiles, send, sent, sems.at[pl.ds(6, 4)])
    for copy in saves:
        copy.wait()


def forward_kernel(core, arrived, matrix_gate, matrix_up, *refs):
    act_out, slope_out, activ_out, act, slope, activ, gate, up, tiles, x_rows, sems = refs[-11:]
    depth = arrived.shape[2]

    def work():
        gate_copy = fetch(matrix_gate, gate, sems.at[0])
        up_copy = fetch(matrix_up, up, sems.at[1])
        untile(arrived[:, 2 * CAP :], tiles, x_rows, depth)
        gate_copy.wait()
        up_copy.wait()
        act[...], slope[...], activ[...] = forward_parts(x_rows, gate, up)
        saves = [
            fetch(act, act_out, sems.at[2]),
            fetch(slope, slope_out, sems.at[3]),
            fetch(activ, activ_out, sems.at[4]),
        ]
        for copy in saves:
            copy.wait()

    pl.when(on_core(core))(work)


def lower_kernel(
    dy_in, act_in, slope_in, own_dt, other_dt, own_gut, other_gut, sent, dy_out,
    dy, act, slope, down_t, gate_up_t, tiles, dy_rows, send, sems,
):
    mine = on_core(0)
    count, depth = send.shape[:2]
    pieces = 4
    part = count // pieces
    arriving = [
        fetch(dy_in.at[pl.ds(n * part, part)], dy.at[pl.ds(n * part, part)], sems.at[9 + n])
        for n in range(pieces)
    ]
    down_copy = fetch_one_of(mine, own_dt, other_dt, down_t, sems.at[0])
    for n, copy in enumerate(arriving):
        copy.wait()
        if n == 1:
            act_copy = fetch(act_in, act, sems.at[1])
            slope_copy = fetch(slope_in, slope, sems.at[2])
            back_copy = fetch_one_of(mine, own_gut, other_gut, gate_up_t, sems.at[3])
        tiles[n * part * depth : (n + 1) * part * depth, :] = (
            dy[n * part : (n + 1) * part].astype(F32).reshape(part * depth, LANES)
        )
    tiles_to_rows(tiles, dy_rows, count, depth)
    saves = [fetch(dy_rows, dy_out, sems.at[4])]
    down_copy.wait()
    grad_act = jnp.dot(dy_rows[...], down_t[...], preferred_element_type=F32)
    for copy in (act_copy, slope_copy, back_copy):
        copy.wait()
    saves += back_part(
        grad_act, act[...], slope[...], gate_up_t, tiles, send, sent, sems.at[pl.ds(5, 4)]
    )
    for copy in saves:
        copy.wait()


INPLACE = pl.BlockSpec(memory_space=pltpu.VMEM)


def placed(arg, spec):
    if spec is HBM:
        return pltpu.with_memory_space_constraint(arg, pltpu.HBM)
    if spec is INPLACE:
        return pltpu.with_memory_space_constraint(arg, pltpu.VMEM)
    return arg


def call(kernel, args, in_specs, out_shape, out_specs, scratch, flops, moved, aliases={}):
    return pl.pallas_call(
        kernel,
        in_specs=in_specs,
        out_shape=tuple(
            pltpu.HBM(out.shape, out.dtype) if spec is HBM else out
            for out, spec in zip(out_shape, out_specs)
        ),
        out_specs=out_specs,
        scratch_shapes=scratch,
        input_output_aliases=aliases,
        compiler_params=pltpu.CompilerParams(vmem_limit_bytes=VMEM_MIB * 1024 * 1024),
        cost_estimate=pl.CostEstimate(flops=flops, bytes_accessed=moved, transcendentals=0),
    )(*[placed(arg, spec) for arg, spec in zip(args, in_specs)])


def swapped(block):
    return lax.ppermute(block, "segment", [(0, 1), (1, 0)])


def exchanged(block):
    return lax.all_to_all(block, "expert", split_axis=0, concat_axis=0, tiled=True)


def shape(dims, kind=BF16):
    return jax.ShapeDtypeStruct(dims, kind)


def shards(saved_input, out_grad, expert_ids, router_weights, w_gate, w_up, w_down, eigenbasis):
    experts = lax.axis_size("expert")
    segment = lax.axis_index("segment")
    upper = segment == 1
    micros, tokens, width = saved_input.shape[1:]
    hidden = w_gate.shape[-1]
    depth = width // LANES
    count = experts * CAP
    gate, up, down, basis = w_gate[0, 0], w_up[0, 0], w_down[0, 0], eigenbasis[0, 0]

    other_x = swapped(
        lax.dynamic_index_in_dim(saved_input[0], 1 - segment, 0, keepdims=False)
    )
    ids = jnp.swapaxes(expert_ids[0], 1, 2)
    own_w = jnp.swapaxes(router_weights[0], 1, 2)
    order = 2 * np.arange(tokens)[None, :] + np.arange(2)[:, None]
    earlier = order[None, None] < order[..., None, None]
    same = ids[:, None, None] == ids[..., None, None]
    rank = jnp.sum((same & earlier[None]).astype(jnp.int32), axis=(3, 4))
    own_slots = ids * CAP + jnp.minimum(rank, CAP - 1)
    other_slots, other_w = swapped(own_slots), swapped(own_w)

    matrix = pltpu.VMEM((width, hidden), BF16)
    turned_shapes = (shape((2 * hidden, width)), shape((width, hidden)))
    turn_scratch = [
        matrix, matrix, pltpu.VMEM((hidden, width), BF16), pltpu.VMEM((2 * hidden, width), BF16),
        matrix, pltpu.SemaphoreType.DMA((5,)),
    ]

    def turned(turn, matrices, made=()):
        return call(
            functools.partial(turn_kernel, turn),
            (*matrices, *made),
            [HBM] * (3 + len(made)),
            turned_shapes,
            (HBM,) * 2,
            turn_scratch,
            1_000_000,
            9_000_000,
            {3: 0, 4: 1} if made else {},
        )

    early_gut, early_dt = turned(0, (gate, up, down))

    tile_rows = tokens * depth
    row_block = pltpu.VMEM((tokens, width), BF16)
    send, grad_tiles = call(
        dispatch_kernel,
        (own_slots, other_slots, own_w, other_w, saved_input[0], other_x, out_grad, early_dt),
        [SMEM] * 4 + [HBM, INPLACE, HBM, HBM],
        (shape((experts, 3 * CAP, depth, LANES)), shape((tokens, depth, LANES))),
        (HBM,) * 2,
        [
            pltpu.VMEM((experts, 3 * CAP, depth, LANES), BF16),
            pltpu.VMEM((tokens, depth, LANES), BF16),
        ]
        + [row_block] * 2
        + [pltpu.VMEM((tile_rows, LANES), F32)] * 3
        + [pltpu.SemaphoreType.DMA((7,))],
        1_000_000,
        5_000_000,
    )
    arrived = exchanged(send)

    own_gut, own_dt = turned(1, (gate, up, down), (early_gut, early_dt))
    other_gate, other_up, other_down = swapped(gate), swapped(up), swapped(down)
    other_basis = swapped(basis)
    other_gut, other_dt = turned(None, (other_gate, other_up, other_down))

    tiles = pltpu.VMEM((count * depth, LANES), F32)
    rows = pltpu.VMEM((count, width), BF16)
    flat = (count, depth, LANES)
    flat_scratch = pltpu.VMEM(flat, BF16)
    mat = 2 * count * width * hidden

    def forwarded(core, matrix_gate, matrix_up, made=()):
        return call(
            functools.partial(forward_kernel, core),
            (arrived, matrix_gate, matrix_up, *made),
            [INPLACE] + [HBM] * (2 + len(made)),
            (shape((count, hidden), F32), shape((count, hidden), F32), shape((count, hidden))),
            (HBM,) * 3,
            [
                pltpu.VMEM((count, hidden), F32), pltpu.VMEM((count, hidden), F32),
                pltpu.VMEM((count, hidden), BF16), matrix, matrix, tiles, rows,
                pltpu.SemaphoreType.DMA((5,)),
            ],
            2 * mat,
            5_000_000,
            {3 + n: n for n in range(len(made))},
        )

    early = forwarded(0, gate, up)
    back_send, dy_rows1, activ1 = call(
        upper_kernel,
        (
            arrived, gate, other_gate, up, other_up, own_dt, other_dt, own_gut, other_gut,
            early[2],
        ),
        [INPLACE] + [HBM] * 9,
        (shape(flat), shape((count, width)), shape((count, hidden))),
        (HBM,) * 3,
        [
            matrix, matrix, matrix, pltpu.VMEM((2 * hidden, width), BF16), tiles,
            rows, rows, pltpu.VMEM((count, hidden), BF16), flat_scratch,
            pltpu.SemaphoreType.DMA((10,)),
        ],
        5 * mat,
        9_000_000,
    )

    def returned(block):
        return exchanged(block.reshape(experts, CAP, depth, LANES)).reshape(flat)

    back = returned(back_send)
    act0, slope0, activ0 = forwarded(1, other_gate, other_up, early)
    basis1 = jnp.where(upper, basis, other_basis)
    basis0 = jnp.where(upper, other_basis, basis)
    rotated1 = jnp.dot(activ1, basis1, preferred_element_type=F32).astype(BF16)
    rotated0 = jnp.dot(activ0, basis0, preferred_element_type=F32).astype(BF16)

    dy_send, grad1 = call(
        relay_kernel,
        (own_slots, other_slots, own_w, other_w, back, grad_tiles),
        [SMEM] * 4 + [INPLACE, VMEM],
        (shape(flat), shape((tokens, depth, LANES))),
        (HBM, HBM),
        [
            flat_scratch, pltpu.VMEM((tokens, depth, LANES), BF16),
            pltpu.SemaphoreType.DMA((2,)),
        ],
        1_000_000,
        3_000_000,
    )
    own_grads, away = call(
        stow_kernel,
        (grad1,),
        [HBM],
        (shape((micros, tokens, width)), shape((tokens, width))),
        (HBM,) * 2,
        [
            pltpu.VMEM((tokens, depth, LANES), BF16), pltpu.VMEM((tile_rows, LANES), F32),
            row_block, pltpu.SemaphoreType.DMA((2,)),
        ],
        1_000_000,
        1_000_000,
    )
    dy = returned(dy_send)
    back_send0, dy_rows0 = call(
        lower_kernel,
        (dy, act0, slope0, own_dt, other_dt, own_gut, other_gut),
        [HBM] * 7,
        (shape(flat), shape((count, width))),
        (HBM,) * 2,
        [
            flat_scratch, pltpu.VMEM((count, hidden), F32), pltpu.VMEM((count, hidden), F32),
            matrix, pltpu.VMEM((2 * hidden, width), BF16), tiles, rows, flat_scratch,
            pltpu.SemaphoreType.DMA((13,)),
        ],
        3 * mat,
        8_000_000,
    )
    back0 = returned(back_send0)

    all_rotated = jnp.concatenate(
        [
            jnp.where(upper, rotated1, rotated0),
            swapped(jnp.where(upper, rotated0, rotated1)),
        ],
        axis=0,
    )
    all_dy = jnp.concatenate(
        [
            jnp.where(upper, dy_rows1, dy_rows0),
            swapped(jnp.where(upper, dy_rows0, dy_rows1)),
        ],
        axis=0,
    )
    rot_sq = (all_rotated.astype(F32) ** 2).astype(BF16)
    dy_sq = (all_dy.astype(F32) ** 2).astype(BF16)
    over_rows = (((0,), (0,)), ((), ()))
    grad_sum = lax.dot_general(all_rotated, all_dy, over_rows, preferred_element_type=F32)
    scale_sum = lax.dot_general(rot_sq, dy_sq, over_rows, preferred_element_type=F32)
    rotated_grad = (grad_sum * (1.0 / micros)).astype(BF16)
    ekfac_scales = scale_sum * (1.0 / micros)
    back0, rotated_grad, ekfac_scales = lax.optimization_barrier(
        (back0, rotated_grad, ekfac_scales)
    )

    def finished(core, made):
        (out,) = call(
            functools.partial(finish_kernel, core),
            (own_slots, other_slots, back0, grad1, made),
            [HBM, HBM, INPLACE, HBM, HBM],
            (shape(made.shape),),
            (HBM,),
            [
                pltpu.SMEM((micros, 2, tokens), jnp.int32),
                pltpu.SMEM((micros, 2, tokens), jnp.int32),
                pltpu.VMEM((tokens, depth, LANES), BF16),
                pltpu.VMEM((tile_rows, LANES), F32),
                row_block,
                pltpu.SemaphoreType.DMA((4,)),
            ],
            3_000_000_000,
            2_000_000,
            {4: 0},
        )
        return out

    came = swapped(finished(1, away))
    own_grads = finished(0, own_grads)
    (grads,) = call(
        join_kernel,
        (came, own_grads),
        [INPLACE, HBM],
        (shape((micros, tokens, width)),),
        (HBM,),
        [pltpu.SemaphoreType.DMA((1,))],
        0,
        1_000_000,
        {1: 0},
    )
    return (grads[None], rotated_grad[None, None], ekfac_scales[None, None])


def solution(mesh):
    in_specs = (
        P("segment", None, "expert", None),
        P(None, "expert", None),
        P("segment", None, "expert", None),
        P("segment", None, "expert", None),
        P("segment", "expert", None, None),
        P("segment", "expert", None, None),
        P("segment", "expert", None, None),
        P("segment", "expert", None, None),
    )
    out_specs = (
        P("segment", None, "expert", None),
        P("segment", "expert", None, None),
        P("segment", "expert", None, None),
    )
    return jax.shard_map(shards, mesh=mesh, in_specs=in_specs, out_specs=out_specs, check_vma=False)
```
